32 devices in a mesh: ctx: 8 (over z, y), dp: 4 (over x, core).
Axes of the slice: x: 2, y: 2, z: 4, core: 2. Of those that a mesh axis runs over, the one named last changes fastest.
Arguments:
- queries: bfloat16 [4, 4096, 512], P('dp', 'ctx'), may hold values from -40 to 40
- keys: bfloat16 [4, 4096, 512], P('dp', 'ctx'), may hold values from -40 to 40
- values: bfloat16 [4, 4096, 512], P('dp', 'ctx'), may hold values from -6 to 6
- segment_ids: int32 [4, 4096], P('dp', 'ctx'), may hold values from 0 to 7, never falling along the last dimension, each value on 1 to 1024 neighbouring positions
- out_grad: bfloat16 [4, 4096, 2048], P('dp', 'ctx'), may hold values from -6 to 6
- out_weight: bfloat16 [512, 2048], replicated, may hold values from -0.25 to 0.25
Outputs:
- query_grad: bfloat16 [4, 4096, 512], P('dp', 'ctx')
- key_grad: bfloat16 [4, 4096, 512], P('dp', 'ctx')
- value_grad: bfloat16 [4, 4096, 512], P('dp', 'ctx')
- weight_grad: float32 [512, 2048], P('ctx', 'dp')
The draws below stay inside these ranges and needn't reach their ends.
Inputs may be any that keep to these rules, and one draw needn't show every extreme that they name: `segment_ids`: segment numbers never fall along a sequence; every segment holds 1 to 1024 positions, and some segment exactly 1024.
All inputs are finite; a program needn't handle non-finite values.
Results may differ from the reference program's by a relative error of at most 0.0096.
Values may be sent and summed in bfloat16 or wider, within the bound.
No kernel may reach another device: no remote copies, remote signals or barrier semaphores. Data moves between devices by JAX's collectives and lax.ppermute only.
A program may use at most 128 MiB of HBM per device.

```python
import math
import jax
import jax.numpy as jnp
import numpy as np
from jax import lax

D = 2048
HEADS = 8
HEAD_DIM = 64
TOK_DEV = 512
SPAN = 2
HD = 512
LENGTH = 4096
BATCH = 4
SEG_MAX = 1024
SEGMENTS = 8


def query_key_pair(key):
    base = jax.random.fold_in(key, 7301)
    first, second = jax.random.split(base, 2)
    shape = (BATCH, LENGTH, HEADS * HEAD_DIM)
    query_draw = jax.random.normal(first, shape, jnp.float32)
    key_draw = jax.random.normal(second, shape, jnp.float32)
    return (jnp.clip(query_draw, -40.0, 40.0), jnp.clip(key_draw, -40.0, 40.0))


def draw_queries(key, part):
    return query_key_pair(key)[0].astype(jnp.bfloat16)


def draw_keys(key, part):
    return query_key_pair(key)[1].astype(jnp.bfloat16)


def levels(key, shape, cuts, smallest, high):
    gain = 1.0
    for dim, parts in cuts:
        steps = jax.random.uniform(jax.random.fold_in(jax.random.fold_in(key, 6), dim), (parts,), jnp.float32, smallest / len(cuts), high / len(cuts))
        gain = gain * jnp.repeat(jnp.exp(steps), shape[dim] // parts).reshape((-1,) + (1,) * (len(shape) - 1 - dim))
    return gain


def length_profile(count, total, bound, lean):
    portions = [(1 << 20) // math.isqrt(standing ** lean) + 1 for standing in range(2, count + 1)]
    spare, counts = total - bound - (count - 1), [1] * (count - 1)
    while spare > 0:
        movable = [i for i in range(count - 1) if counts[i] < bound]
        whole, left = sum([portions[i] for i in movable]), spare
        for i in movable:
            addition = min(bound - counts[i], max(1, left * portions[i] // whole), spare)
            counts[i] = counts[i] + addition
            spare = spare - addition
    return np.array([bound] + counts)


def ragged_sizes(own_key, amount, total, limit, slope):
    if amount == 2:
        one = jax.random.randint(own_key, (), max(1, total - limit), min(limit, total - 1) + 1)
        return jnp.stack([one, total - one])
    lengths = jnp.asarray(length_profile(amount, total, limit, slope), jnp.int32)
    couples = (amount - 1) // 2
    source_of, sink = lengths[1:1 + 2 * couples:2], lengths[2:2 + 2 * couples:2]
    margin = jnp.minimum(source_of - 1, limit - sink)
    moved = jax.random.randint(jax.random.fold_in(own_key, 1), (couples,), 0, 1 << 20) % (margin + 1)
    lengths = lengths.at[1:1 + 2 * couples:2].set(source_of - moved).at[2:2 + 2 * couples:2].set(sink + moved)
    return lengths[jax.random.permutation(jax.random.fold_in(own_key, 2), amount)]


def normal_values(own_key, extent, deviation, limit, shards=(), kind=jnp.bfloat16):
    values = deviation * jax.random.normal(own_key, extent, jnp.float32)
    if shards:
        values = values * levels(own_key, extent, shards, -0.22, 0.18)
    return jnp.clip(values, -limit, limit).astype(kind)


def setup_inputs(seed: int = 0) -> dict:
    splits = jax.random.split(jax.random.key(seed), 7)
    queries = draw_queries(jax.random.fold_in(splits[6], 71), 0)
    keys = draw_keys(jax.random.fold_in(splits[6], 71), 0)
    values = normal_values(splits[2], (BATCH, LENGTH, HD), 1.0, 6.0, ((0, 4), (1, 8)))
    segment_ids = jax.vmap(lambda own: jnp.searchsorted(jnp.cumsum(ragged_sizes(own, SEGMENTS, LENGTH, SEG_MAX, 2)), jnp.arange(LENGTH), side="right"))(jax.random.split(splits[3], BATCH)).reshape((BATCH, LENGTH)).astype(jnp.int32)
    out_grad = normal_values(splits[4], (BATCH, LENGTH, D), 1.0, 6.0, ((0, 4), (1, 8)))
    out_weight = normal_values(splits[5], (HD, D), HD ** -0.5, 0.25)
    return {"queries": queries, "keys": keys, "values": values, "segment_ids": segment_ids, "out_grad": out_grad, "out_weight": out_weight}


MASKED_SCORE = -1.0e30


def one_sequence(query_seq, key_seq, value_seq, segment_seq, grad_seq, out_weight):
    width = SPAN * TOK_DEV
    block_count = LENGTH // TOK_DEV
    score_scale = HEAD_DIM ** -0.5
    attn_grad = jnp.dot(grad_seq, out_weight.T, preferred_element_type=jnp.float32).astype(jnp.bfloat16)
    query_float = query_seq.astype(jnp.float32).reshape(LENGTH, HEADS, HEAD_DIM)
    key_float = jnp.concatenate([jnp.zeros((width, HD), jnp.float32), key_seq.astype(jnp.float32)]).reshape(LENGTH + width, HEADS, HEAD_DIM)
    value_float = jnp.concatenate([jnp.zeros((width, HD), jnp.float32), value_seq.astype(jnp.float32)]).reshape(LENGTH + width, HEADS, HEAD_DIM)
    segment_pad = jnp.concatenate([jnp.full((width,), -1, jnp.int32), segment_seq.astype(jnp.int32)])
    grad_float = attn_grad.astype(jnp.float32).reshape(LENGTH, HEADS, HEAD_DIM)

    def advance(carried, block_id):
        key_total, value_total, weight_total = carried
        first_row = (block_id * TOK_DEV).astype(jnp.int32)
        query_part = lax.dynamic_slice_in_dim(query_float, first_row, TOK_DEV, 0)
        grad_part = lax.dynamic_slice_in_dim(grad_float, first_row, TOK_DEV, 0)
        out_part = lax.dynamic_slice_in_dim(grad_seq, first_row, TOK_DEV, 0)
        key_part = lax.dynamic_slice_in_dim(key_float, first_row, width + TOK_DEV, 0)
        value_part = lax.dynamic_slice_in_dim(value_float, first_row, width + TOK_DEV, 0)
        query_segment = lax.dynamic_slice_in_dim(segment_seq.astype(jnp.int32), first_row, TOK_DEV, 0)
        key_segment = lax.dynamic_slice_in_dim(segment_pad, first_row, width + TOK_DEV, 0)
        query_pos = first_row + jnp.arange(TOK_DEV, dtype=jnp.int32)
        key_pos = first_row - width + jnp.arange(width + TOK_DEV, dtype=jnp.int32)
        allowed = (query_segment[:, None] == key_segment[None, :]) & (key_pos[None, :] <= query_pos[:, None])
        scores = jnp.einsum("qhd,khd->hqk", query_part, key_part) * score_scale
        scores = jnp.where(allowed[None], scores, MASKED_SCORE)
        row_peak = jnp.max(scores, axis=-1, keepdims=True)
        log_total = row_peak + jnp.log(jnp.sum(jnp.exp(scores - row_peak), axis=-1, keepdims=True))
        prob_float = jnp.exp(scores - log_total)
        prob_half = lax.optimization_barrier(prob_float.astype(jnp.bfloat16))
        prob_back = prob_half.astype(jnp.float32)
        attn_float = jnp.einsum("hqk,khd->qhd", prob_back, value_part)
        attn_half = attn_float.reshape(TOK_DEV, HD).astype(jnp.bfloat16)
        row_delta = jnp.einsum("qhd,qhd->hq", grad_part, attn_float)[:, :, None]
        prob_grad = jnp.einsum("qhd,khd->hqk", grad_part, value_part)
        score_grad = lax.optimization_barrier((prob_float * (prob_grad - row_delta) * score_scale).astype(jnp.bfloat16))
        score_back = score_grad.astype(jnp.float32)
        query_out = jnp.einsum("hqk,khd->qhd", score_back, key_part).reshape(TOK_DEV, HD).astype(jnp.bfloat16)
        key_term = jnp.einsum("hqk,qhd->khd", score_back, query_part).reshape(width + TOK_DEV, HD)
        value_term = jnp.einsum("hqk,qhd->khd", prob_back, grad_part).reshape(width + TOK_DEV, HD)
        key_total = lax.dynamic_update_slice_in_dim(key_total, lax.dynamic_slice_in_dim(key_total, first_row, width + TOK_DEV, 0) + key_term, first_row, 0)
        value_total = lax.dynamic_update_slice_in_dim(value_total, lax.dynamic_slice_in_dim(value_total, first_row, width + TOK_DEV, 0) + value_term, first_row, 0)
        weight_total = weight_total + jnp.dot(attn_half.T, out_part, preferred_element_type=jnp.float32)
        return (key_total, value_total, weight_total), query_out

    start_state = (jnp.zeros((LENGTH + width, HD), jnp.float32), jnp.zeros((LENGTH + width, HD), jnp.float32), jnp.zeros((HD, D), jnp.float32))
    final_state, query_blocks = lax.scan(advance, start_state, jnp.arange(block_count, dtype=jnp.int32))
    key_total, value_total, weight_total = final_state
    return query_blocks.reshape(LENGTH, HD), key_total[width:].astype(jnp.bfloat16), value_total[width:].astype(jnp.bfloat16), weight_total


def reference(queries, keys, values, segment_ids, out_grad, out_weight):
    query_list = []
    key_list = []
    value_list = []
    weight_grad = jnp.zeros((HD, D), jnp.float32)
    for seq_id in range(BATCH):
        query_out, key_out, value_out, weight_part = one_sequence(queries[seq_id], keys[seq_id], values[seq_id], segment_ids[seq_id], out_grad[seq_id], out_weight)
        query_list.append(query_out)
        key_list.append(key_out)
        value_list.append(value_out)
        weight_grad = weight_grad + weight_part
    return (jnp.stack(query_list), jnp.stack(key_list), jnp.stack(value_list), weight_grad)
```

```python
import functools

import jax
import jax.numpy as jnp
from jax import lax
from jax.experimental import pallas as pl
from jax.experimental.pallas import tpu as pltpu
from jax.sharding import PartitionSpec as P

HEAD_DIM = 64
TILE = 256
LANES = 128
TAG_LANES = 64
PIECES = 3
MASKED_SCORE = -1e30
SCALE = HEAD_DIM ** (-0.5)
F32 = jnp.float32
BF16 = jnp.bfloat16
PARAMS = pltpu.CompilerParams(vmem_limit_bytes=20 << 20)


def shift(x, by):
    size = lax.axis_size("ctx")
    pairs = [(i, i + by) for i in range(size) if 0 <= i + by < size]
    return lax.ppermute(x, "ctx", pairs)


def dot_t(a, b):
    return lax.dot_general(a, b, (((1,), (1,)), ((), ())), preferred_element_type=F32)


def dot(a, b):
    return jnp.dot(a, b, preferred_element_type=F32)


def lane_of(rows):
    return lax.broadcasted_iota(jnp.int32, (rows, LANES), 1)


def one_hot(tag_row):
    count = tag_row.shape[1]
    tag = lax.broadcasted_iota(jnp.int32, (LANES, count), 0) + 1
    hit = (tag_row.astype(F32) == tag.astype(F32)) & (tag <= TAG_LANES)
    return jnp.where(hit, 1.0, 0.0).astype(F32).T


def key_extra(tag_row):
    hot = one_hot(tag_row)
    lane = lane_of(hot.shape[0])
    return jnp.where(lane < TAG_LANES, (1.0 - hot) * MASKED_SCORE, 1.0).astype(BF16)


def pieces(x):
    out = []
    for _ in range(PIECES):
        part = x.astype(BF16).astype(F32)
        out.append(part)
        x = x - part
    return out


def own(lane, half):
    return (lane >= half * HEAD_DIM) & (lane < (half + 1) * HEAD_DIM)


def query_extra(stats, head):
    lane = lane_of(stats.shape[0])
    first = TAG_LANES + 2 * PIECES * head
    none = jnp.zeros_like(stats)
    tag_lse = (lane < TAG_LANES) | ((lane >= first) & (lane < first + PIECES))
    delta = (lane >= first + PIECES) & (lane < first + 2 * PIECES)
    return jnp.where(tag_lse, stats, none), jnp.where(delta, stats, none)


def wide(features, extra):
    return jnp.concatenate([features, extra], axis=1)


def lower(shape, by_query):
    a = lax.broadcasted_iota(jnp.int32, shape, 0)
    b = lax.broadcasted_iota(jnp.int32, shape, 1)
    return (b <= a) if by_query else (a <= b)


def forward_kernel(first_pair, q_ref, g_ref, kc, vc, ka, va, kb, vb, tc, ta, tb, *rest):
    before = rest[0] if first_pair else None
    o_ref, st_ref, xc, xa, xb, tag, rowed = rest[1 if first_pair else 0 :]
    step = pl.program_id(0)
    rows = q_ref.shape[0]

    @pl.when(step == 0)
    def _():
        xc[...] = key_extra(tc[...])
        xa[...] = key_extra(ta[0:1, :])
        xb[...] = key_extra(tb[0:1, :])
        tag[...] = one_hot(tc[...]).astype(BF16)
        rowed[...] = jnp.zeros_like(rowed)

    lane = lane_of(TILE)
    vt = {id(v): v[...].T for v in (va, vb, vc)}
    gt = g_ref[...].T.astype(F32)
    for base in range(0, rows, TILE):
        end = base + TILE
        spans = [(ka, va, xa, base, rows), (kb, vb, xb, 0, rows)]
        spans += [(kc, vc, xc, 0, base)] if base else []
        spans += [(kc, vc, xc, base, end)]
        q = q_ref[base:end, :] * SCALE
        for half in range(2):
            feats = slice(half * HEAD_DIM, (half + 1) * HEAD_DIM)
            qx = wide(jnp.where(own(lane, half), q, jnp.zeros_like(q)), tag[base:end, :])
            scores = [dot_t(wide(k[lo:hi, :], x[lo:hi, :]), qx) for k, v, x, lo, hi in spans]
            scores[-1] = jnp.where(lower((TILE, TILE), False), scores[-1], MASKED_SCORE)
            peak = functools.reduce(
                jnp.maximum, [jnp.max(s, axis=0, keepdims=True) for s in scores]
            )
            total = jnp.zeros((1, TILE), F32)
            acc = jnp.zeros((HEAD_DIM, TILE), F32)
            for s, (k, v, x, lo, hi) in zip(scores, spans):
                e = jnp.exp(s - peak)
                total = total + jnp.sum(e, axis=0, keepdims=True)
                acc = acc + dot(vt[id(v)][feats, lo:hi], e.astype(BF16))
            acc = acc / total
            o_ref[feats, base:end] = acc.astype(BF16)
            delta = jnp.sum(acc * gt[feats, base:end], axis=0, keepdims=True)
            first = TAG_LANES + 2 * PIECES * (2 * (step + first_pair) + half)
            for i, part in enumerate(pieces(-(peak + jnp.log(total))) + pieces(-delta)):
                rowed[pl.ds(first + i, 1), base:end] = part

    @pl.when(step == pl.num_programs(0) - 1)
    def _():
        was = tag[...] if before is None else before[...]
        st_ref[...] = (was.astype(F32) + rowed[...].T).astype(BF16)


def query_kernel(first_pair, q_ref, g_ref, st_ref, kc, vc, ka, va, kb, vb, tc, ta, tb, *rest):
    dq_ref, xc, xa, xb, acc = rest[1 if first_pair else 0 :]
    step = pl.program_id(0)
    rows = q_ref.shape[0]

    @pl.when(step == 0)
    def _():
        xc[...] = key_extra(tc[...])
        xa[...] = key_extra(ta[0:1, :])
        xb[...] = key_extra(tb[0:1, :])

    lane = lane_of(rows)
    q = q_ref[...] * SCALE
    g = g_ref[...]
    for half in range(2):
        mine = own(lane, half)
        for_score, for_grad = query_extra(st_ref[...], 2 * (step + first_pair) + half)
        qx = wide(jnp.where(mine, q, jnp.zeros_like(q)), for_score)
        gx = wide(jnp.where(mine, g, jnp.zeros_like(g)), for_grad)
        acc[...] = jnp.zeros_like(acc)
        for k, v, x, near in ((ka, va, xa, 0), (kb, vb, xb, 1), (kc, vc, xc, 2)):
            for lo in range(0, rows, TILE):
                hi = lo + TILE
                top = lo if near == 2 else 0
                end = hi if near == 0 else rows
                p = jnp.exp(dot_t(qx[top:end], wide(k[lo:hi, :], x[lo:hi, :])))
                if near == 2:
                    p = jnp.where(lower((end - top, TILE), True), p, 0.0)
                dp = dot_t(gx[top:end], wide(v[lo:hi, :], x[lo:hi, :]))
                acc[top:end, :] += dot((p * dp).astype(BF16), k[lo:hi, :])
        if half == 0:
            dq_ref[...] = (acc[...] * SCALE).astype(BF16)
        else:
            dq_ref[...] = jnp.where(mine, (acc[...] * SCALE).astype(BF16), dq_ref[...])


def key_kernel(first_pair, k_ref, v_ref, t_ref, qc, gc, sc, qd, gd, sd, qe, ge, se, *rest):
    dk_ref, dv_ref, x_ref, dk, dv = rest[2 if first_pair else 0 :]
    step = pl.program_id(0)
    rows = k_ref.shape[0]

    @pl.when(step == 0)
    def _():
        x_ref[...] = key_extra(t_ref[...])

    lane = lane_of(TILE)
    kx = wide(k_ref[...], x_ref[...])
    vx = wide(v_ref[...], x_ref[...])
    for half in range(2):
        dk[...] = jnp.zeros_like(dk)
        dv[...] = jnp.zeros_like(dv)
        mine = own(lane, half)
        for q_ref, g_ref, s_ref, near in ((qc, gc, sc, 2), (qd, gd, sd, 1), (qe, ge, se, 0)):
            for lo in range(0, rows, TILE):
                hi = lo + TILE
                top = lo if near == 0 else 0
                end = hi if near == 2 else rows
                q = q_ref[lo:hi, :] * SCALE
                g = g_ref[lo:hi, :]
                for_score, for_grad = query_extra(s_ref[lo:hi, :], 2 * (step + first_pair) + half)
                qx = wide(jnp.where(mine, q, jnp.zeros_like(q)), for_score)
                gx = wide(jnp.where(mine, g, jnp.zeros_like(g)), for_grad)
                p = jnp.exp(dot_t(kx[top:end], qx))
                if near == 2:
                    row = lax.broadcasted_iota(jnp.int32, p.shape, 0)
                    col = lax.broadcasted_iota(jnp.int32, p.shape, 1) + lo
                    p = jnp.where(row <= col, p, 0.0)
                dp = dot_t(vx[top:end], gx)
                dv[top:end, :] += dot(p.astype(BF16), g)
                dk[top:end, :] += dot((p * dp).astype(BF16), q)
        if half == 0:
            dk_ref[...] = dk[...].astype(BF16)
            dv_ref[...] = dv[...].astype(BF16)
        else:
            keep = own(lane_of(rows), half)
            dk_ref[...] = jnp.where(keep, dk[...].astype(BF16), dk_ref[...])
            dv_ref[...] = jnp.where(keep, dv[...].astype(BF16), dv_ref[...])


def lasting(microseconds):
    return pl.CostEstimate(flops=0, transcendentals=0, bytes_accessed=int(microseconds * 3.5e6))


class Attention:
    def __init__(self, rows, width, chunk, chunks):
        pairs = width // LANES // chunks
        self.first = chunk * pairs
        block = lambda off: pl.BlockSpec((rows, LANES), lambda p: (0, p + off))
        fixed = lambda shape, row: pl.BlockSpec(shape, lambda p: (row, 0))
        here, whole = self.first, width // LANES
        own_tag, far_tag = fixed((1, rows), 0), fixed((16, rows), rows // 16)
        self.stat = stat = fixed((rows, LANES), 0)
        self.sent = sent = [block(here), block(whole + here)]
        self.window = [block(here)] * 2 + [block(0), block(pairs)] * 2 + [own_tag, far_tag, far_tag]
        self.local = [block(here)] * 2 + [own_tag]
        self.out = block(here)
        self.extra = pltpu.VMEM((rows, LANES), BF16)
        self.total = pltpu.VMEM((rows, LANES), F32)
        self.rows, self.width, self.pairs = rows, width, pairs

    def call(self, kernel, in_specs, args, out_specs, out_shape, scratch, before=(), aliased=True, last=8):
        before = list(before)
        spec = pl.BlockSpec(memory_space=pl.ANY) if aliased else self.stat
        aliases = {len(args) + i: i for i in range(len(before))} if aliased else {}
        return pl.pallas_call(
            functools.partial(kernel, self.first), grid=(self.pairs,),
            in_specs=in_specs + [spec] * len(before), out_specs=out_specs,
            out_shape=[jax.ShapeDtypeStruct(s, BF16) for s in out_shape],
            scratch_shapes=scratch, input_output_aliases=aliases,
            compiler_params=PARAMS, cost_estimate=lasting(last), name=kernel.__name__,
        )(*args, *before)

    def forward(self, sent, window, before):
        return self.call(
            forward_kernel, self.sent + self.window, [sent, sent, *window],
            [pl.BlockSpec((LANES, self.rows), lambda p: (p, 0)), self.stat],
            [(self.pairs * LANES, self.rows), (self.rows, LANES)],
            [self.extra] * 4 + [pltpu.VMEM((LANES, self.rows), F32)], before, False,
        )

    def query(self, sent, stats, window, before):
        return self.call(
            query_kernel, self.sent + [self.stat] + self.window, [sent, sent, stats, *window],
            [self.out], [(self.rows, self.width)], [self.extra] * 3 + [self.total], before,
        )

    def key(self, local, sources, before):
        return self.call(
            key_kernel, self.local + (self.sent + [self.stat]) * 3, local + sources,
            [self.out] * 2, [(self.rows, self.width)] * 2, [self.extra] + [self.total] * 2, before,
        )


def send_kernel(q_ref, g_ref, w_ref, out_ref):
    half = pl.num_programs(0) // 2
    step = pl.program_id(0)

    @pl.when(step < half)
    def _():
        out_ref[...] = q_ref[...]

    @pl.when(step >= half)
    def _():
        out_ref[...] = dot_t(g_ref[...], w_ref[...]).astype(BF16)


def queries_to_send(query_rows, grad_rows, out_weight):
    rows, width = query_rows.shape
    model = grad_rows.shape[1]
    blocks = width // TILE
    return pl.pallas_call(
        send_kernel, grid=(2 * blocks,),
        in_specs=[
            pl.BlockSpec((rows, TILE), lambda i: (0, jnp.minimum(i, blocks - 1))),
            pl.BlockSpec((rows, model), lambda i: (0, 0)),
            pl.BlockSpec((TILE, model), lambda i: (jnp.maximum(i - blocks, 0), 0)),
        ],
        out_specs=pl.BlockSpec((rows, TILE), lambda i: (0, i)),
        out_shape=jax.ShapeDtypeStruct((rows, 2 * width), BF16),
        compiler_params=PARAMS, cost_estimate=lasting(5), name="queries_to_send",
    )(query_rows, grad_rows, out_weight)


def weight_kernel(sel_ref, *refs):
    outs, g_ref, w_ref = refs[:2], refs[2], refs[-1]
    size = outs[0].shape[0]
    for i, o_ref in enumerate(outs):
        part = dot(o_ref[...], g_ref[...])
        if len(refs) == 5:
            part = part + refs[3][0, i * size : (i + 1) * size, :].astype(F32)
        w_ref[0, i * size : (i + 1) * size, :] = part.astype(w_ref.dtype)


def weight_term(attn, grad_rows, columns, parts, got, dtype):
    size, rows = attn[0].shape
    width = size * len(attn)
    cols = grad_rows.shape[1] // parts
    steps = 1 if got is not None else parts // 2
    column = lambda i, s: (0, s[0] + 2 * i)
    extra = [] if got is None else [pl.BlockSpec((1, width, cols), lambda i, s: (s[1], 0, 0))]
    return pl.pallas_call(
        weight_kernel,
        grid_spec=pltpu.PrefetchScalarGridSpec(
            num_scalar_prefetch=1, grid=(steps,),
            in_specs=[pl.BlockSpec((size, rows), lambda i, s: (0, 0))] * 2
            + [pl.BlockSpec((rows, cols), column)] + extra,
            out_specs=pl.BlockSpec((1, width, cols), lambda i, s: (i, 0, 0)),
        ),
        out_shape=jax.ShapeDtypeStruct((steps, width, cols), dtype),
        compiler_params=PARAMS, cost_estimate=lasting(3), name="weight_term",
    )(columns, *attn, grad_rows, *([] if got is None else [got]))


def swap(x, axis, bit):
    return lax.ppermute(x, axis, [(i, i ^ bit) for i in range(lax.axis_size(axis))])


def after(x, *others):
    return lax.optimization_barrier((x,) + others)[0]


def weight_by_dp(attn, grad_rows):
    parts = lax.axis_size("dp")
    me = lax.axis_index("dp").astype(jnp.int32)
    core, chip = me % 2, me // 2
    pick = lambda part, entry: jnp.stack([part, entry])
    sent = weight_term(attn, grad_rows, pick(1 - core, core), parts, None, BF16)
    got = swap(sent, "dp", 1)
    sent = weight_term(attn, grad_rows, pick(2 * (1 - chip) + core, 1 - chip), parts, got, BF16)
    moved = swap(sent, "dp", 2)
    kept = weight_term(attn, grad_rows, pick(me, chip), parts, got, F32)
    return kept[0], moved[0]


def halves(total, got, axis, bit):
    split = lambda x: x.reshape((x.shape[0] // 2, 2) + x.shape[1:])
    total, got = split(total), split(got)
    mine = (lax.axis_index(axis) // bit) % 2
    take = lambda which: lax.dynamic_index_in_dim(
        total, which, 1, keepdims=False
    ) + lax.dynamic_index_in_dim(got, which, 1, keepdims=False).astype(F32)
    return take(1 - mine).astype(BF16), take(mine)


def on_device(queries, keys, values, segment_ids, out_grad, out_weight):
    query_rows, key_rows, value_rows, grad_rows = queries[0], keys[0], values[0], out_grad[0]
    rows, width = query_rows.shape
    chunks = 2
    size = width // chunks
    tags = segment_ids + 1
    tag_rows = jnp.pad(tags.astype(BF16), ((0, 15), (0, 2 * size - rows)))
    odd = lax.axis_index("ctx") % 2 == 1
    mine, far = [], []
    for i in range(chunks):
        cut = slice(i * size, (i + 1) * size)
        mine.append(
            jnp.concatenate(
                [jnp.concatenate([key_rows[:, cut], value_rows[:, cut]], axis=1), tag_rows], axis=0
            )
        )
        far.append(shift(mine[i], 2))
    sent = queries_to_send(after(query_rows, *mine), grad_rows, out_weight)
    far_sent = shift(sent, -2)
    far[0] = after(far[0], sent)
    near = []
    for i in range(chunks):
        passed = jnp.where(odd, far[i], mine[i])
        near.append(swap(passed, "ctx", 1))
        if i + 1 < chunks:
            far[i + 1] = after(far[i + 1], passed)
    parts = [Attention(rows, width, i, chunks) for i in range(chunks)]
    window = lambda i: [key_rows, value_rows, far[i], far[i], near[i], near[i], tags, far[i], near[i]]
    attn, stats = [], []
    from_forward = sent
    for i in range(chunks):
        half, after_half = parts[i].forward(from_forward, window(i), stats)
        attn.append(half)
        stats = [after_half]
        if i == 0:
            passed = jnp.where(odd, sent, after(far_sent, half))
            near_sent = swap(passed, "ctx", 1)
            from_forward = after(sent, passed)
    stats = stats[0]
    kept, moved = weight_by_dp(attn, grad_rows)
    near_stats = shift(stats, -1)
    far_stats = shift(stats, -2)
    settled = [stats, after(stats, near_stats, far_stats)]
    query_grad = []
    for i in range(chunks):
        query_grad = parts[i].query(sent, settled[i], window(i), query_grad)
    query_grad = query_grad[0]
    by_ctx = lambda x: x.reshape(count, width // count, x.shape[-1])
    count = lax.axis_size("ctx")
    kept, moved = by_ctx(kept), by_ctx(moved)
    key_value = []
    sources = [sent, sent, stats, near_sent, near_sent, near_stats, far_sent, far_sent, far_stats]
    bit = 1
    chunk = 0
    moved = after(moved, query_grad)
    while bit < count:
        send, kept = halves(kept, moved, "ctx", bit)
        moved = swap(send, "ctx", bit)
        if chunk < chunks:
            tied, send = lax.optimization_barrier((stats, send))
            sources[2] = tied
            key_value = parts[chunk].key([key_rows, value_rows, tags], sources, key_value)
            moved = after(moved, *key_value)
            chunk += 1
        bit *= 2
    weight_grad = kept[0] + moved[0].astype(F32)
    key_grad, value_grad = key_value
    return query_grad[None], key_grad[None], value_grad[None], weight_grad


def solution(mesh):
    rows = P("dp", "ctx", None)
    return jax.shard_map(
        on_device,
        mesh=mesh,
        in_specs=(rows, rows, rows, P("dp", "ctx"), rows, P()),
        out_specs=(rows, rows, rows, P("ctx", "dp")),
        check_vma=False,
    )
```

```python
import functools

import jax
import jax.numpy as jnp
from jax import lax
from jax.experimental import pallas as pl
from jax.experimental.pallas import tpu as pltpu
from jax.sharding import PartitionSpec as P

HEAD_DIM = 64
TILE = 256
LANES = 128
TAG_LANES = 64
PIECES = 3
MASKED_SCORE = -1e30
SCALE = HEAD_DIM ** (-0.5)
F32 = jnp.float32
BF16 = jnp.bfloat16
PARAMS = pltpu.CompilerParams(vmem_limit_bytes=16 << 20)


def shift(x, by):
    size = lax.axis_size("ctx")
    pairs = [(i, i + by) for i in range(size) if 0 <= i + by < size]
    return lax.ppermute(x, "ctx", pairs)


def dot_t(a, b):
    return lax.dot_general(a, b, (((1,), (1,)), ((), ())), preferred_element_type=F32)


def dot(a, b):
    return jnp.dot(a, b, preferred_element_type=F32)


def lane_of(rows):
    return lax.broadcasted_iota(jnp.int32, (rows, LANES), 1)


def one_hot(tag_row):
    count = tag_row.shape[1]
    tag = lax.broadcasted_iota(jnp.int32, (LANES, count), 0) + 1
    hit = (tag_row.astype(F32) == tag.astype(F32)) & (tag <= TAG_LANES)
    return jnp.where(hit, 1.0, 0.0).astype(F32).T


def key_extra(tag_row):
    hot = one_hot(tag_row)
    lane = lane_of(hot.shape[0])
    return jnp.where(lane < TAG_LANES, (1.0 - hot) * MASKED_SCORE, 1.0).astype(BF16)


def pieces(x):
    out = []
    for _ in range(PIECES):
        part = x.astype(BF16).astype(F32)
        out.append(part)
        x = x - part
    return out


def own(lane, half):
    return (lane >= half * HEAD_DIM) & (lane < (half + 1) * HEAD_DIM)


def factor(chosen, value=1.0):
    return jnp.where(chosen, value, 0.0).astype(F32).astype(BF16)


def own_factor(half, value=1.0):
    return factor(own(lane_of(1), half), value)


def extra_factors(head):
    lane = lane_of(1)
    first = TAG_LANES + 2 * PIECES * head
    tag_lse = (lane < TAG_LANES) | ((lane >= first) & (lane < first + PIECES))
    delta = (lane >= first + PIECES) & (lane < first + 2 * PIECES)
    return factor(tag_lse), factor(delta)


def wide(features, extra):
    return jnp.concatenate([features, extra], axis=1)


def lower(shape, by_query):
    a = lax.broadcasted_iota(jnp.int32, shape, 0)
    b = lax.broadcasted_iota(jnp.int32, shape, 1)
    return (b <= a) if by_query else (a <= b)


def join(to_k, to_v, to_x, ke, ve, te, ko, vo, to, first_step):
    to_k[...] = ke[...] + ko[...]
    to_v[...] = ve[...] + vo[...]

    @pl.when(first_step)
    def _():
        to_x[...] = key_extra(te[0:1, :] + to[0:1, :])


def forward_kernel(first_pair, q_ref, g_ref, kc, vc, tc, ka, va, ta, ke, ve, te, ko, vo, to, *rest):
    before = rest[0] if first_pair else None
    o_ref, st_ref, xc, xa, xb, kb, vb, tag, rowed = rest[1 if first_pair else 0 :]
    step = pl.program_id(0)
    rows = q_ref.shape[0]

    @pl.when(step == 0)
    def _():
        xc[...] = key_extra(tc[0:1, :])
        xa[...] = key_extra(ta[0:1, :])
        tag[...] = one_hot(tc[0:1, :]).astype(BF16)
        rowed[...] = jnp.zeros_like(rowed)

    join(kb, vb, xb, ke, ve, te, ko, vo, to, step == 0)

    vt = {id(v): v[...].T for v in (va, vb, vc)}
    gt = g_ref[...].T.astype(F32)
    for base in range(0, rows, TILE):
        end = base + TILE
        spans = [(ka, va, xa, base, rows), (kb, vb, xb, 0, rows)]
        spans += [(kc, vc, xc, 0, base)] if base else []
        spans += [(kc, vc, xc, base, end)]
        q = q_ref[base:end, :]
        for half in range(2):
            feats = slice(half * HEAD_DIM, (half + 1) * HEAD_DIM)
            qx = wide(q * own_factor(half, SCALE), tag[base:end, :])
            scores = [dot_t(wide(k[lo:hi, :], x[lo:hi, :]), qx) for k, v, x, lo, hi in spans]
            scores[-1] = jnp.where(lower((TILE, TILE), False), scores[-1], MASKED_SCORE)
            peak = functools.reduce(
                jnp.maximum, [jnp.max(s, axis=0, keepdims=True) for s in scores]
            )
            total = jnp.zeros((1, TILE), F32)
            acc = jnp.zeros((HEAD_DIM, TILE), F32)
            for s, (k, v, x, lo, hi) in zip(scores, spans):
                e = jnp.exp(s - peak)
                total = total + jnp.sum(e, axis=0, keepdims=True)
                acc = acc + dot(vt[id(v)][feats, lo:hi], e.astype(BF16))
            acc = acc / total
            o_ref[feats, base:end] = acc.astype(BF16)
            delta = jnp.sum(acc * gt[feats, base:end], axis=0, keepdims=True)
            first = TAG_LANES + 2 * PIECES * (2 * (step + first_pair) + half)
            for i, part in enumerate(pieces(-(peak + jnp.log(total))) + pieces(-delta)):
                rowed[pl.ds(first + i, 1), base:end] = part

    @pl.when(step == pl.num_programs(0) - 1)
    def _():
        was = tag[...] if before is None else before[...]
        st_ref[...] = (was.astype(F32) + rowed[...].T).astype(BF16)


def query_kernel(first_pair, q_ref, g_ref, st_ref, kc, vc, tc, ka, va, ta, ke, ve, te, ko, vo, to, *rest):
    dq_ref, xc, xa, xb, kb, vb, acc, first = rest[1 if first_pair else 0 :]
    step = pl.program_id(0)
    rows = q_ref.shape[0]

    @pl.when(step == 0)
    def _():
        xc[...] = key_extra(tc[0:1, :])
        xa[...] = key_extra(ta[0:1, :])

    join(kb, vb, xb, ke, ve, te, ko, vo, to, step == 0)
    lane = lane_of(rows)
    q, g, stats = q_ref[...], g_ref[...], st_ref[...]
    for half in range(2):
        mine = own(lane, half)
        for_score, for_grad = extra_factors(2 * (step + first_pair) + half)
        qx = wide(q * own_factor(half, SCALE), stats * for_score)
        gx = wide(g * own_factor(half), stats * for_grad)
        acc[...] = jnp.zeros_like(acc)
        for k, v, x, near in ((ka, va, xa, 0), (kb, vb, xb, 1), (kc, vc, xc, 2)):
            for lo in range(0, rows, TILE):
                hi = lo + TILE
                top = lo if near == 2 else 0
                end = hi if near == 0 else rows
                p = jnp.exp(dot_t(qx[top:end], wide(k[lo:hi, :], x[lo:hi, :])))
                if near == 2:
                    p = jnp.where(lower((end - top, TILE), True), p, 0.0)
                dp = dot_t(gx[top:end], wide(v[lo:hi, :], x[lo:hi, :]))
                acc[top:end, :] += dot((p * dp).astype(BF16), k[lo:hi, :])
        if half == 0:
            first[...] = acc[...]
        else:
            dq_ref[...] = (jnp.where(mine, acc[...], first[...]) * SCALE).astype(BF16)


def key_kernel(first_pair, k_ref, v_ref, t_ref, qc, gc, sc, qd, gd, sd, qe, ge, se, *rest):
    dk_ref, dv_ref, x_ref = rest[2 if first_pair else 0 :][:3]
    dks, dvs = rest[-4:-2], rest[-2:]
    step = pl.program_id(0)
    rows = k_ref.shape[0]

    @pl.when(step == 0)
    def _():
        x_ref[...] = key_extra(t_ref[0:1, :])

    kx = wide(k_ref[...], x_ref[...])
    vx = wide(v_ref[...], x_ref[...])
    for half in range(2):
        dk, dv = dks[half], dvs[half]
        dk[...] = jnp.zeros_like(dk)
        dv[...] = jnp.zeros_like(dv)
        for_score, for_grad = extra_factors(2 * (step + first_pair) + half)
        for q_ref, g_ref, s_ref, near in ((qc, gc, sc, 2), (qd, gd, sd, 1), (qe, ge, se, 0)):
            for lo in range(0, rows, TILE):
                hi = lo + TILE
                top = lo if near == 0 else 0
                end = hi if near == 2 else rows
                q, g, stats = q_ref[lo:hi, :], g_ref[lo:hi, :], s_ref[lo:hi, :]
                qx = wide(q * own_factor(half, SCALE), stats * for_score)
                gx = wide(g * own_factor(half), stats * for_grad)
                p = jnp.exp(dot_t(kx[top:end], qx))
                if near == 2:
                    row = lax.broadcasted_iota(jnp.int32, p.shape, 0)
                    col = lax.broadcasted_iota(jnp.int32, p.shape, 1) + lo
                    p = jnp.where(row <= col, p, 0.0)
                dp = dot_t(vx[top:end], gx)
                dv[top:end, :] += dot(p.astype(BF16), g)
                dk[top:end, :] += dot((p * dp).astype(BF16), q)
    second = own(lane_of(rows), 1)
    dk_ref[...] = (jnp.where(second, dks[1][...], dks[0][...]) * SCALE).astype(BF16)
    dv_ref[...] = jnp.where(second, dvs[1][...], dvs[0][...]).astype(BF16)


def lasting(microseconds):
    return pl.CostEstimate(flops=0, transcendentals=0, bytes_accessed=int(microseconds * 3.5e6))


class Attention:
    def __init__(self, rows, width, chunks, first, count):
        whole = width // LANES
        size = whole // chunks
        begin = first // size * size
        block = lambda off: pl.BlockSpec((rows, LANES), lambda p: (0, p + off))
        tag = pl.BlockSpec((16, rows), lambda p: (rows // 16, 0))
        self.first, self.count, self.rows, self.width = first, count, rows, width
        self.stat = pl.BlockSpec((rows, LANES), lambda p: (0, 0))
        self.sent = [block(first), block(whole + first)]
        self.held = [block(first - begin), block(size + first - begin), tag]
        self.out = block(first)
        self.extra = pltpu.VMEM((rows, LANES), BF16)
        self.total = pltpu.VMEM((rows, LANES), F32)

    def call(self, kernel, in_specs, args, out_specs, out_shape, scratch, before, aliased, last):
        before = list(before)
        spec = pl.BlockSpec(memory_space=pl.ANY) if aliased else self.stat
        aliases = {len(args) + i: i for i in range(len(before))} if aliased else {}
        return pl.pallas_call(
            functools.partial(kernel, self.first), grid=(self.count,),
            in_specs=in_specs + [spec] * len(before), out_specs=out_specs,
            out_shape=[jax.ShapeDtypeStruct(s, BF16) for s in out_shape],
            scratch_shapes=scratch, input_output_aliases=aliases,
            compiler_params=PARAMS, cost_estimate=lasting(last * self.count), name=kernel.__name__,
        )(*args, *before)

    def forward(self, sent, window, before):
        return self.call(
            forward_kernel, self.sent + self.held * 4,
            [sent, sent] + [x for x in window for _ in range(3)],
            [pl.BlockSpec((LANES, self.rows), lambda p: (p, 0)), self.stat],
            [(self.count * LANES, self.rows), (self.rows, LANES)],
            [self.extra] * 6 + [pltpu.VMEM((LANES, self.rows), F32)], before, False, 3.5,
        )

    def query(self, sent, stats, window, before):
        return self.call(
            query_kernel, self.sent + [self.stat] + self.held * 4,
            [sent, sent, stats] + [x for x in window for _ in range(3)],
            [self.out], [(self.rows, self.width)], [self.extra] * 5 + [self.total] * 2, before, True, 3.5,
        )

    def key(self, held, sources, before):
        return self.call(
            key_kernel, self.held + (self.sent + [self.stat]) * 3,
            [held] * 3 + [in_hbm(x) for q, st in sources for x in (q, q, st)],
            [self.out] * 2, [(self.rows, self.width)] * 2, [self.extra] + [self.total] * 4,
            before, True, 4.2,
        )


def send_kernel(q_ref, g_ref, w_ref, out_ref):
    half = pl.num_programs(0) // 2
    step = pl.program_id(0)

    @pl.when(step < half)
    def _():
        out_ref[...] = q_ref[...]

    @pl.when(step >= half)
    def _():
        out_ref[...] = dot_t(g_ref[...], w_ref[...]).astype(BF16)


def queries_to_send(query_rows, grad_rows, out_weight):
    rows, width = query_rows.shape
    model = grad_rows.shape[1]
    blocks = width // TILE
    return pl.pallas_call(
        send_kernel, grid=(2 * blocks,),
        in_specs=[
            pl.BlockSpec((rows, TILE), lambda i: (0, jnp.minimum(i, blocks - 1))),
            pl.BlockSpec((rows, model), lambda i: (0, 0)),
            pl.BlockSpec((TILE, model), lambda i: (jnp.maximum(i - blocks, 0), 0)),
        ],
        out_specs=pl.BlockSpec((rows, TILE), lambda i: (0, i)),
        out_shape=jax.ShapeDtypeStruct((rows, 2 * width), BF16),
        compiler_params=PARAMS, cost_estimate=lasting(5), name="queries_to_send",
    )(query_rows, grad_rows, out_weight)


def weight_kernel(sel_ref, *refs):
    outs, g_ref, w_ref = refs[:2], refs[2], refs[-1]
    size = outs[0].shape[0]
    for i, o_ref in enumerate(outs):
        part = dot(o_ref[...], g_ref[...])
        if len(refs) == 5:
            part = part + refs[3][0, i * size : (i + 1) * size, :].astype(F32)
        w_ref[0, i * size : (i + 1) * size, :] = part.astype(w_ref.dtype)


def weight_term(attn, grad_rows, columns, parts, got, dtype):
    size, rows = attn[0].shape
    width = size * len(attn)
    cols = grad_rows.shape[1] // parts
    steps = 1 if got is not None else parts // 2
    column = lambda i, s: (0, s[0] + 2 * i)
    extra = [] if got is None else [pl.BlockSpec((1, width, cols), lambda i, s: (s[1], 0, 0))]
    return pl.pallas_call(
        weight_kernel,
        grid_spec=pltpu.PrefetchScalarGridSpec(
            num_scalar_prefetch=1, grid=(steps,),
            in_specs=[pl.BlockSpec((size, rows), lambda i, s: (0, 0))] * 2
            + [pl.BlockSpec((rows, cols), column)] + extra,
            out_specs=pl.BlockSpec((1, width, cols), lambda i, s: (i, 0, 0)),
        ),
        out_shape=jax.ShapeDtypeStruct((steps, width, cols), dtype),
        compiler_params=PARAMS, cost_estimate=lasting(3), name="weight_term",
    )(columns, *map(in_hbm, attn), in_hbm(grad_rows), *([] if got is None else [got]))


def keep_kernel(sel_ref, o0_ref, o1_ref, g_ref, got_ref, moved_ref, send_ref, keep_ref):
    mine = sel_ref[2]
    count, size = send_ref.shape[0], send_ref.shape[1]
    half = o0_ref.shape[0]
    for i, o_ref in enumerate((o0_ref, o1_ref)):
        cut = slice(i * half, (i + 1) * half)
        part = dot(o_ref[...], g_ref[...]) + got_ref[0, cut, :].astype(F32) + moved_ref[0, cut, :].astype(F32)
        part = part.reshape(count // 2, 2, size, part.shape[1])
        low, high = part[:, 0], part[:, 1]
        out = slice(i * count // 2, (i + 1) * count // 2)
        send_ref[out] = jnp.where(mine == 0, high, low).astype(BF16)
        keep_ref[out] = jnp.where(mine == 0, low, high)


def keep_term(attn, grad_rows, columns, parts, got, moved, blocks):
    size, rows = attn[0].shape
    width = size * len(attn)
    cols = grad_rows.shape[1] // parts
    shape = (blocks // 2, width // blocks, cols)
    fixed = lambda shape: pl.BlockSpec(shape, lambda i, s: (0,) * len(shape))
    return pl.pallas_call(
        keep_kernel,
        grid_spec=pltpu.PrefetchScalarGridSpec(
            num_scalar_prefetch=1, grid=(1,),
            in_specs=[fixed((size, rows))] * 2 + [
                pl.BlockSpec((rows, cols), lambda i, s: (0, s[0])),
                pl.BlockSpec((1, width, cols), lambda i, s: (s[1], 0, 0)),
                fixed((1, width, cols)),
            ],
            out_specs=[fixed(shape)] * 2,
        ),
        out_shape=[jax.ShapeDtypeStruct(shape, BF16), jax.ShapeDtypeStruct(shape, F32)],
        compiler_params=PARAMS, cost_estimate=lasting(3), name="keep_term",
    )(columns, *map(in_hbm, attn), in_hbm(grad_rows), got, moved)


def swap(x, axis, bit):
    return lax.ppermute(x, axis, [(i, i ^ bit) for i in range(lax.axis_size(axis))])


def within_pair(x, to_odd):
    size = lax.axis_size("ctx")
    return lax.ppermute(x, "ctx", [(i, i + 1) if to_odd else (i + 1, i) for i in range(0, size, 2)])


def in_hbm(x):
    return pltpu.with_memory_space_constraint(x, pltpu.HBM)


def after(x, *others):
    return lax.optimization_barrier((x,) + others)[0]


def whole_of(x):
    return pl.BlockSpec(x.shape, lambda i, s: (0,) * x.ndim)


def stage_kernel(sel_ref, total_ref, got_ref, send_ref, keep_ref):
    mine = sel_ref[0]
    total = total_ref[...] + got_ref[...].astype(F32)
    total = total.reshape((send_ref.shape[0], 2) + send_ref.shape[1:])
    low, high = total[:, 0], total[:, 1]
    send_ref[...] = jnp.where(mine == 0, high, low).astype(BF16)
    keep_ref[...] = jnp.where(mine == 0, low, high)


def halves(total, got, axis, bit):
    mine = ((lax.axis_index(axis) // bit) % 2).astype(jnp.int32).reshape(1)
    out = lambda dtype: jax.ShapeDtypeStruct((total.shape[0] // 2,) + total.shape[1:], dtype)
    return pl.pallas_call(
        stage_kernel,
        grid_spec=pltpu.PrefetchScalarGridSpec(
            num_scalar_prefetch=1, grid=(1,), in_specs=[whole_of(total), whole_of(got)],
            out_specs=[whole_of(out(F32))] * 2,
        ),
        out_shape=[out(BF16), out(F32)],
        compiler_params=PARAMS, cost_estimate=lasting(1), name="stage",
    )(mine, total, got)


def last_kernel(total_ref, got_ref, out_ref):
    out_ref[...] = total_ref[...] + got_ref[...].astype(F32)


def last_sum(total, got):
    return pl.pallas_call(
        last_kernel, out_shape=jax.ShapeDtypeStruct(total.shape, F32),
        compiler_params=PARAMS, cost_estimate=lasting(1), name="last_sum",
    )(total, got)


def on_device(queries, keys, values, segment_ids, out_grad, out_weight):
    query_rows, key_rows, value_rows, grad_rows = queries[0], keys[0], values[0], out_grad[0]
    rows, width = query_rows.shape
    pairs = width // LANES
    chunks = 2
    size = width // chunks
    tag_rows = jnp.pad((segment_ids + 1).astype(BF16), ((0, 15), (0, 2 * size - rows)))
    odd = lax.axis_index("ctx") % 2 == 1
    mine, far, paired, passed = [], [], [], []
    for i in range(chunks):
        cut = slice(i * size, (i + 1) * size)
        mine.append(
            jnp.concatenate(
                [jnp.concatenate([key_rows[:, cut], value_rows[:, cut]], axis=1), tag_rows], axis=0
            )
        )
        far.append(shift(mine[i], 2))
    sent = queries_to_send(after(query_rows, *mine), grad_rows, out_weight)
    far[0] = after(far[0], sent)
    for i in range(chunks):
        paired.append(within_pair(mine[i], True))
        passed.append(within_pair(far[i], False))
    far_sent = shift(sent, -2)
    parts = [Attention(rows, width, chunks, i * pairs // chunks, pairs // chunks) for i in range(chunks)]
    window = lambda i: [mine[i], far[i], paired[i], passed[i]]
    attn, stats = [], []
    from_forward = sent
    for i in range(chunks):
        half, after_half = parts[i].forward(from_forward, window(i), stats)
        attn.append(half)
        stats = [after_half]
        if i == 0:
            relayed = jnp.where(odd, sent, after(far_sent, half))
            near_sent = swap(relayed, "ctx", 1)
            from_forward = after(sent, relayed)
    stats = stats[0]
    near_stats = shift(stats, -1)
    far_stats = shift(stats, -2)

    shares = lax.axis_size("dp")
    count = lax.axis_size("ctx")
    me = lax.axis_index("dp").astype(jnp.int32)
    core, chip = me % 2, me // 2
    low = lax.axis_index("ctx").astype(jnp.int32) % 2
    pick = lambda part, entry: jnp.stack([part, entry, low])
    got = swap(weight_term(attn, grad_rows, pick(1 - core, core), shares, None, BF16), "dp", 1)
    to_chip = weight_term(attn, grad_rows, pick(2 * (1 - chip) + core, 1 - chip), shares, got, BF16)
    moved = swap(to_chip, "dp", 2)
    query_grad = []
    for i in range(chunks):
        query_grad = parts[i].query(sent, stats, window(i), query_grad)
    query_grad = query_grad[0]
    moved = after(moved, query_grad, near_stats, far_stats)
    send, kept = keep_term(attn, grad_rows, pick(me, chip), shares, got, moved, count)

    pieces_of_keys = [(0, 2), (2, 1), (3, 1)]
    key_value = []
    stage = 0
    bit = 1
    while bit < count:
        moved = swap(send, "ctx", bit)
        if stage < len(pieces_of_keys):
            first, some = pieces_of_keys[stage]
            tied, send = lax.optimization_barrier((stats, send))
            sources = [(sent, tied), (near_sent, near_stats), (far_sent, far_stats)]
            held = mine[first * chunks // pairs]
            key_value = Attention(rows, width, chunks, first, some).key(held, sources, key_value)
            moved = after(moved, *key_value)
            stage += 1
        bit *= 2
        if bit < count:
            send, kept = halves(kept, moved, "ctx", bit)
    weight_grad = last_sum(kept[0], moved[0])
    key_grad, value_grad = key_value
    return query_grad[None], key_grad[None], value_grad[None], weight_grad


def solution(mesh):
    rows = P("dp", "ctx", None)
    return jax.shard_map(
        on_device,
        mesh=mesh,
        in_specs=(rows, rows, rows, P("dp", "ctx"), rows, P()),
        out_specs=(rows, rows, rows, P("ctx", "dp")),
        check_vma=False,
    )
```

```python
import functools

import jax
import jax.numpy as jnp
from jax import lax
from jax.experimental import pallas as pl
from jax.experimental.pallas import tpu as pltpu
from jax.sharding import PartitionSpec as P

HEAD_DIM = 64
TILE = 256
LANES = 128
TAG_LANES = 64
PIECES = 3
MASKED_SCORE = -1e30
SCALE = HEAD_DIM ** (-0.5)
F32 = jnp.float32
BF16 = jnp.bfloat16
PARAMS = pltpu.CompilerParams(vmem_limit_bytes=16 << 20)


def shift(x, by):
    size = lax.axis_size("ctx")
    pairs = [(i, i + by) for i in range(size) if 0 <= i + by < size]
    return lax.ppermute(x, "ctx", pairs)


def dot_t(a, b):
    return lax.dot_general(a, b, (((1,), (1,)), ((), ())), preferred_element_type=F32)


def dot(a, b):
    return jnp.dot(a, b, preferred_element_type=F32)


def lane_of(rows):
    return lax.broadcasted_iota(jnp.int32, (rows, LANES), 1)


def one_hot(tag_row):
    count = tag_row.shape[1]
    tag = lax.broadcasted_iota(jnp.int32, (LANES, count), 0) + 1
    hit = (tag_row.astype(F32) == tag.astype(F32)) & (tag <= TAG_LANES)
    return jnp.where(hit, 1.0, 0.0).astype(F32).T


def key_extra(tag_row):
    hot = one_hot(tag_row)
    lane = lane_of(hot.shape[0])
    return jnp.where(lane < TAG_LANES, (1.0 - hot) * MASKED_SCORE, 1.0).astype(BF16)


def pieces(x):
    out = []
    for _ in range(PIECES):
        part = x.astype(BF16).astype(F32)
        out.append(part)
        x = x - part
    return out


def own(lane, half):
    return (lane >= half * HEAD_DIM) & (lane < (half + 1) * HEAD_DIM)


def factor(chosen, value=1.0):
    return jnp.where(chosen, value, 0.0).astype(F32).astype(BF16)


def own_factor(half, value=1.0):
    return factor(own(lane_of(1), half), value)


def extra_factors(head):
    lane = lane_of(1)
    first = TAG_LANES + 2 * PIECES * head
    tag_lse = (lane < TAG_LANES) | ((lane >= first) & (lane < first + PIECES))
    delta = (lane >= first + PIECES) & (lane < first + 2 * PIECES)
    return factor(tag_lse), factor(delta)


def wide(features, extra):
    return jnp.concatenate([features, extra], axis=1)


def lower(shape, by_query):
    a = lax.broadcasted_iota(jnp.int32, shape, 0)
    b = lax.broadcasted_iota(jnp.int32, shape, 1)
    return (b <= a) if by_query else (a <= b)


def join(to_k, to_v, to_x, ke, ve, te, ko, vo, to, first_step):
    to_k[...] = ke[...] + ko[...]
    to_v[...] = ve[...] + vo[...]

    @pl.when(first_step)
    def _():
        to_x[...] = key_extra(te[0:1, :] + to[0:1, :])


def forward_kernel(first_pair, q_ref, g_ref, kc, vc, tc, ka, va, ta, ke, ve, te, ko, vo, to, *rest):
    before = rest[0] if first_pair else None
    o_ref, st_ref, xc, xa, xb, kb, vb, tag, rowed = rest[1 if first_pair else 0 :]
    step = pl.program_id(0)
    rows = q_ref.shape[0]

    @pl.when(step == 0)
    def _():
        xc[...] = key_extra(tc[0:1, :])
        xa[...] = key_extra(ta[0:1, :])
        tag[...] = one_hot(tc[0:1, :]).astype(BF16)
        rowed[...] = jnp.zeros_like(rowed)

    join(kb, vb, xb, ke, ve, te, ko, vo, to, step == 0)

    lane = lane_of(TILE)
    fold = lambda op, arrays: functools.reduce(
        op, [x[:, i : i + LANES] for x in arrays for i in range(0, x.shape[1], LANES)]
    )
    def score(base, half):
        end = base + TILE
        spans = [(ka, va, xa, base, rows), (kb, vb, xb, 0, rows)]
        spans += [(kc, vc, xc, 0, base)] if base else []
        spans += [(kc, vc, xc, base, end)]
        qx = wide(q_ref[base:end, :] * own_factor(half, SCALE), tag[base:end, :])
        scores = [dot_t(qx, wide(k[lo:hi, :], x[lo:hi, :])) for k, v, x, lo, hi in spans]
        scores[-1] = jnp.where(lower((TILE, TILE), True), scores[-1], MASKED_SCORE)
        return scores, spans

    turns = [(base, half) for base in range(0, rows, TILE) for half in range(2)]
    ahead = score(*turns[0])
    outs = []
    for turn, (base, half) in enumerate(turns):
        end = base + TILE
        scores, spans = ahead
        if turn + 1 < len(turns):
            ahead = score(*turns[turn + 1])
        mine = own(lane, half)
        peak = jnp.max(fold(jnp.maximum, scores), axis=1, keepdims=True)
        es = [jnp.exp(s - peak) for s in scores]
        total = jnp.sum(fold(jnp.add, es), axis=1, keepdims=True)
        acc = jnp.zeros((TILE, LANES), F32)
        for e, (k, v, x, lo, hi) in zip(es, spans):
            acc = acc + dot(e.astype(BF16), v[lo:hi, :])
        acc = acc * (1.0 / total)
        g = g_ref[base:end, :].astype(F32)
        delta = jnp.sum(jnp.where(mine, acc * g, 0.0), axis=1, keepdims=True)
        raw = raw if half else jnp.zeros((TILE, LANES), F32)
        for i, column in enumerate((peak, total, delta)):
            raw = jnp.where(lane == 3 * half + i, column, raw)
        outs.append(acc)
        if half == 0:
            continue
        o_ref[:, base:end] = jnp.where(own(lane, 0), outs[-2], outs[-1]).T.astype(BF16)
        turned = raw.T
        for side in range(2):
            peak, total, delta = (turned[3 * side + i : 3 * side + i + 1, :] for i in range(3))
            first = TAG_LANES + 2 * PIECES * (2 * (step + first_pair) + side)
            for i, part in enumerate(pieces(-(peak + jnp.log(total))) + pieces(-delta)):
                rowed[pl.ds(first + i, 1), base:end] = part

    @pl.when(step == pl.num_programs(0) - 1)
    def _():
        was = tag[...] if before is None else before[...]
        st_ref[...] = (was.astype(F32) + rowed[...].T).astype(BF16)


def query_kernel(first_pair, q_ref, g_ref, st_ref, kc, vc, tc, ka, va, ta, ke, ve, te, ko, vo, to, *rest):
    dq_ref, xc, xa, xb, kb, vb, acc, first = rest[1 if first_pair else 0 :]
    step = pl.program_id(0)
    rows = q_ref.shape[0]

    @pl.when(step == 0)
    def _():
        xc[...] = key_extra(tc[0:1, :])
        xa[...] = key_extra(ta[0:1, :])

    join(kb, vb, xb, ke, ve, te, ko, vo, to, step == 0)
    lane = lane_of(rows)
    q, g, stats = q_ref[...], g_ref[...], st_ref[...]
    for half in range(2):
        mine = own(lane, half)
        for_score, for_grad = extra_factors(2 * (step + first_pair) + half)
        qx = wide(q * own_factor(half, SCALE), stats * for_score)
        gx = wide(g * own_factor(half), stats * for_grad)
        acc[...] = jnp.zeros_like(acc)
        turns = [
            (k, v, x, near, lo)
            for k, v, x, near in ((ka, va, xa, 0), (kb, vb, xb, 1), (kc, vc, xc, 2))
            for lo in range(0, rows, TILE)
        ]

        def products(k, v, x, near, lo):
            hi = lo + TILE
            top = lo if near == 2 else 0
            end = hi if near == 0 else rows
            s = dot_t(qx[top:end], wide(k[lo:hi, :], x[lo:hi, :]))
            return s, dot_t(gx[top:end], wide(v[lo:hi, :], x[lo:hi, :])), top, end

        ahead = products(*turns[0])
        for turn, (k, v, x, near, lo) in enumerate(turns):
            s, dp, top, end = ahead
            if turn + 1 < len(turns):
                ahead = products(*turns[turn + 1])
            p = jnp.exp(s)
            if near == 2:
                p = jnp.where(lower((end - top, TILE), True), p, 0.0)
            acc[top:end, :] += dot((p * dp).astype(BF16), k[lo : lo + TILE, :])
        if half == 0:
            first[...] = acc[...]
        else:
            dq_ref[...] = (jnp.where(mine, acc[...], first[...]) * SCALE).astype(BF16)


def key_kernel(first_pair, k_ref, v_ref, t_ref, qc, gc, sc, qd, gd, sd, qe, ge, se, *rest):
    dk_ref, dv_ref, x_ref = rest[2 if first_pair else 0 :][:3]
    dks, dvs = rest[-4:-2], rest[-2:]
    step = pl.program_id(0)
    rows = k_ref.shape[0]

    @pl.when(step == 0)
    def _():
        x_ref[...] = key_extra(t_ref[0:1, :])

    kx = wide(k_ref[...], x_ref[...])
    vx = wide(v_ref[...], x_ref[...])
    for half in range(2):
        dk, dv = dks[half], dvs[half]
        dk[...] = jnp.zeros_like(dk)
        dv[...] = jnp.zeros_like(dv)
        for_score, for_grad = extra_factors(2 * (step + first_pair) + half)
        turns = [
            (q_ref, g_ref, s_ref, near, lo)
            for q_ref, g_ref, s_ref, near in ((qc, gc, sc, 2), (qd, gd, sd, 1), (qe, ge, se, 0))
            for lo in range(0, rows, TILE)
        ]

        def products(q_ref, g_ref, s_ref, near, lo):
            hi = lo + TILE
            top = lo if near == 0 else 0
            end = hi if near == 2 else rows
            q, g, stats = q_ref[lo:hi, :], g_ref[lo:hi, :], s_ref[lo:hi, :]
            qx = wide(q * own_factor(half, SCALE), stats * for_score)
            gx = wide(g * own_factor(half), stats * for_grad)
            return dot_t(kx[top:end], qx), dot_t(vx[top:end], gx), q, g, top, end

        ahead = products(*turns[0])
        for turn, (q_ref, g_ref, s_ref, near, lo) in enumerate(turns):
            s, dp, q, g, top, end = ahead
            if turn + 1 < len(turns):
                ahead = products(*turns[turn + 1])
            p = jnp.exp(s)
            if near == 2:
                row = lax.broadcasted_iota(jnp.int32, p.shape, 0)
                col = lax.broadcasted_iota(jnp.int32, p.shape, 1) + lo
                p = jnp.where(row <= col, p, 0.0)
            dv[top:end, :] += dot(p.astype(BF16), g)
            dk[top:end, :] += dot((p * dp).astype(BF16), q)
    second = own(lane_of(rows), 1)
    dk_ref[...] = (jnp.where(second, dks[1][...], dks[0][...]) * SCALE).astype(BF16)
    dv_ref[...] = jnp.where(second, dvs[1][...], dvs[0][...]).astype(BF16)


def lasting(microseconds):
    return pl.CostEstimate(flops=0, transcendentals=0, bytes_accessed=int(microseconds * 3.5e6))


class Attention:
    def __init__(self, rows, width, chunks, first, count):
        whole = width // LANES
        size = whole // chunks
        begin = first // size * size
        block = lambda off: pl.BlockSpec((rows, LANES), lambda p: (0, p + off))
        tag = pl.BlockSpec((16, rows), lambda p: (rows // 16, 0))
        self.first, self.count, self.rows, self.width = first, count, rows, width
        self.stat = pl.BlockSpec((rows, LANES), lambda p: (0, 0))
        self.sent = [block(first), block(whole + first)]
        self.held = [block(first - begin), block(size + first - begin), tag]
        self.out = block(first)
        self.extra = pltpu.VMEM((rows, LANES), BF16)
        self.total = pltpu.VMEM((rows, LANES), F32)

    def call(self, kernel, in_specs, args, out_specs, out_shape, scratch, before, aliased, last):
        before = list(before)
        spec = pl.BlockSpec(memory_space=pl.ANY) if aliased else self.stat
        aliases = {len(args) + i: i for i in range(len(before))} if aliased else {}
        return pl.pallas_call(
            functools.partial(kernel, self.first), grid=(self.count,),
            in_specs=in_specs + [spec] * len(before), out_specs=out_specs,
            out_shape=[jax.ShapeDtypeStruct(s, BF16) for s in out_shape],
            scratch_shapes=scratch, input_output_aliases=aliases,
            compiler_params=PARAMS, cost_estimate=lasting(last * self.count), name=kernel.__name__,
        )(*args, *before)

    def forward(self, sent, window, before):
        return self.call(
            forward_kernel, self.sent + self.held * 4,
            [sent, sent] + [x for x in window for _ in range(3)],
            [pl.BlockSpec((LANES, self.rows), lambda p: (p, 0)), self.stat],
            [(self.count * LANES, self.rows), (self.rows, LANES)],
            [self.extra] * 6 + [pltpu.VMEM((LANES, self.rows), F32)], before, False, 3.5,
        )

    def query(self, sent, stats, window, before):
        return self.call(
            query_kernel, self.sent + [self.stat] + self.held * 4,
            [sent, sent, stats] + [x for x in window for _ in range(3)],
            [self.out], [(self.rows, self.width)], [self.extra] * 5 + [self.total] * 2, before, True, 3.5,
        )

    def key(self, held, sources, before):
        return self.call(
            key_kernel, self.held + (self.sent + [self.stat]) * 3,
            [held] * 3 + [in_hbm(x) for q, st in sources for x in (q, q, st)],
            [self.out] * 2, [(self.rows, self.width)] * 2, [self.extra] + [self.total] * 4,
            before, True, 4.2,
        )


def send_kernel(q_ref, g_ref, w_ref, out_ref):
    half = pl.num_programs(0) // 2
    step = pl.program_id(0)

    @pl.when(step < half)
    def _():
        out_ref[...] = q_ref[...]

    @pl.when(step >= half)
    def _():
        out_ref[...] = dot_t(g_ref[...], w_ref[...]).astype(BF16)


def queries_to_send(query_rows, grad_rows, out_weight):
    rows, width = query_rows.shape
    model = grad_rows.shape[1]
    blocks = width // TILE
    return pl.pallas_call(
        send_kernel, grid=(2 * blocks,),
        in_specs=[
            pl.BlockSpec((rows, TILE), lambda i: (0, jnp.minimum(i, blocks - 1))),
            pl.BlockSpec((rows, model), lambda i: (0, 0)),
            pl.BlockSpec((TILE, model), lambda i: (jnp.maximum(i - blocks, 0), 0)),
        ],
        out_specs=pl.BlockSpec((rows, TILE), lambda i: (0, i)),
        out_shape=jax.ShapeDtypeStruct((rows, 2 * width), BF16),
        compiler_params=PARAMS, cost_estimate=lasting(5), name="queries_to_send",
    )(query_rows, grad_rows, out_weight)


def weight_kernel(sel_ref, *refs):
    outs, g_ref, w_ref = refs[:2], refs[2], refs[-1]
    size = outs[0].shape[0]
    for i, o_ref in enumerate(outs):
        part = dot(o_ref[...], g_ref[...])
        if len(refs) == 5:
            part = part + refs[3][0, i * size : (i + 1) * size, :].astype(F32)
        w_ref[0, i * size : (i + 1) * size, :] = part.astype(w_ref.dtype)


def weight_term(attn, grad_rows, columns, parts, got, dtype):
    size, rows = attn[0].shape
    width = size * len(attn)
    cols = grad_rows.shape[1] // parts
    steps = 1 if got is not None else parts // 2
    column = lambda i, s: (0, s[0] + 2 * i)
    extra = [] if got is None else [pl.BlockSpec((1, width, cols), lambda i, s: (s[1], 0, 0))]
    return pl.pallas_call(
        weight_kernel,
        grid_spec=pltpu.PrefetchScalarGridSpec(
            num_scalar_prefetch=1, grid=(steps,),
            in_specs=[pl.BlockSpec((size, rows), lambda i, s: (0, 0))] * 2
            + [pl.BlockSpec((rows, cols), column)] + extra,
            out_specs=pl.BlockSpec((1, width, cols), lambda i, s: (i, 0, 0)),
        ),
        out_shape=jax.ShapeDtypeStruct((steps, width, cols), dtype),
        compiler_params=PARAMS, cost_estimate=lasting(3), name="weight_term",
    )(columns, *map(in_hbm, attn), in_hbm(grad_rows), *([] if got is None else [got]))


def keep_kernel(sel_ref, o0_ref, o1_ref, g_ref, got_ref, moved_ref, send_ref, keep_ref):
    mine = sel_ref[2]
    count, size = send_ref.shape[0], send_ref.shape[1]
    half = o0_ref.shape[0]
    for i, o_ref in enumerate((o0_ref, o1_ref)):
        cut = slice(i * half, (i + 1) * half)
        part = dot(o_ref[...], g_ref[...]) + got_ref[0, cut, :].astype(F32) + moved_ref[0, cut, :].astype(F32)
        part = part.reshape(count // 2, 2, size, part.shape[1])
        low, high = part[:, 0], part[:, 1]
        out = slice(i * count // 2, (i + 1) * count // 2)
        send_ref[out] = jnp.where(mine == 0, high, low).astype(BF16)
        keep_ref[out] = jnp.where(mine == 0, low, high)


def keep_term(attn, grad_rows, columns, parts, got, moved, blocks):
    size, rows = attn[0].shape
    width = size * len(attn)
    cols = grad_rows.shape[1] // parts
    shape = (blocks // 2, width // blocks, cols)
    fixed = lambda shape: pl.BlockSpec(shape, lambda i, s: (0,) * len(shape))
    return pl.pallas_call(
        keep_kernel,
        grid_spec=pltpu.PrefetchScalarGridSpec(
            num_scalar_prefetch=1, grid=(1,),
            in_specs=[fixed((size, rows))] * 2 + [
                pl.BlockSpec((rows, cols), lambda i, s: (0, s[0])),
                pl.BlockSpec((1, width, cols), lambda i, s: (s[1], 0, 0)),
                fixed((1, width, cols)),
            ],
            out_specs=[fixed(shape)] * 2,
        ),
        out_shape=[jax.ShapeDtypeStruct(shape, BF16), jax.ShapeDtypeStruct(shape, F32)],
        compiler_params=PARAMS, cost_estimate=lasting(3), name="keep_term",
    )(columns, *map(in_hbm, attn), in_hbm(grad_rows), got, moved)


def swap(x, axis, bit):
    return lax.ppermute(x, axis, [(i, i ^ bit) for i in range(lax.axis_size(axis))])


def within_pair(x, to_odd):
    size = lax.axis_size("ctx")
    return lax.ppermute(x, "ctx", [(i, i + 1) if to_odd else (i + 1, i) for i in range(0, size, 2)])


def in_hbm(x):
    return pltpu.with_memory_space_constraint(x, pltpu.HBM)


def after(x, *others):
    return lax.optimization_barrier((x,) + others)[0]


def whole_of(x):
    return pl.BlockSpec(x.shape, lambda i, s: (0,) * x.ndim)


def stage_kernel(sel_ref, total_ref, got_ref, send_ref, keep_ref):
    mine = sel_ref[0]
    total = total_ref[...] + got_ref[...].astype(F32)
    total = total.reshape((send_ref.shape[0], 2) + send_ref.shape[1:])
    low, high = total[:, 0], total[:, 1]
    send_ref[...] = jnp.where(mine == 0, high, low).astype(BF16)
    keep_ref[...] = jnp.where(mine == 0, low, high)


def halves(total, got, axis, bit):
    mine = ((lax.axis_index(axis) // bit) % 2).astype(jnp.int32).reshape(1)
    out = lambda dtype: jax.ShapeDtypeStruct((total.shape[0] // 2,) + total.shape[1:], dtype)
    return pl.pallas_call(
        stage_kernel,
        grid_spec=pltpu.PrefetchScalarGridSpec(
            num_scalar_prefetch=1, grid=(1,), in_specs=[whole_of(total), whole_of(got)],
            out_specs=[whole_of(out(F32))] * 2,
        ),
        out_shape=[out(BF16), out(F32)],
        compiler_params=PARAMS, cost_estimate=lasting(1), name="stage",
    )(mine, total, got)


def last_kernel(total_ref, got_ref, out_ref):
    out_ref[...] = total_ref[...] + got_ref[...].astype(F32)


def last_sum(total, got):
    return pl.pallas_call(
        last_kernel, out_shape=jax.ShapeDtypeStruct(total.shape, F32),
        compiler_params=PARAMS, cost_estimate=lasting(1), name="last_sum",
    )(total, got)


def on_device(queries, keys, values, segment_ids, out_grad, out_weight):
    query_rows, key_rows, value_rows, grad_rows = queries[0], keys[0], values[0], out_grad[0]
    rows, width = query_rows.shape
    pairs = width // LANES
    chunks = 2
    size = width // chunks
    tag_rows = jnp.pad((segment_ids + 1).astype(BF16), ((0, 15), (0, 2 * size - rows)))
    odd = lax.axis_index("ctx") % 2 == 1
    mine, far, paired, passed = [], [], [], []
    for i in range(chunks):
        cut = slice(i * size, (i + 1) * size)
        tagged = after(tag_rows, *mine)
        mine.append(
            jnp.concatenate(
                [jnp.concatenate([key_rows[:, cut], value_rows[:, cut]], axis=1), tagged], axis=0
            )
        )
        far.append(shift(mine[i], 2))
    sent = queries_to_send(after(query_rows, *mine), grad_rows, out_weight)
    far[0] = after(far[0], sent)
    for i in range(chunks):
        paired.append(within_pair(mine[i], True))
        passed.append(within_pair(far[i], False))
    far_sent = shift(sent, -2)
    parts = [Attention(rows, width, chunks, i * pairs // chunks, pairs // chunks) for i in range(chunks)]
    window = lambda i: [mine[i], far[i], paired[i], passed[i]]
    attn, stats = [], []
    from_forward = sent
    for i in range(chunks):
        half, after_half = parts[i].forward(from_forward, window(i), stats)
        attn.append(half)
        stats = [after_half]
        if i == 0:
            relayed = jnp.where(odd, sent, after(far_sent, half))
            near_sent = swap(relayed, "ctx", 1)
            from_forward = after(sent, relayed)
    stats = stats[0]
    near_stats = shift(stats, -1)
    far_stats = shift(stats, -2)

    shares = lax.axis_size("dp")
    count = lax.axis_size("ctx")
    me = lax.axis_index("dp").astype(jnp.int32)
    core, chip = me % 2, me // 2
    low = lax.axis_index("ctx").astype(jnp.int32) % 2
    pick = lambda part, entry: jnp.stack([part, entry, low])
    got = swap(weight_term(attn, grad_rows, pick(1 - core, core), shares, None, BF16), "dp", 1)
    to_chip = weight_term(attn, grad_rows, pick(2 * (1 - chip) + core, 1 - chip), shares, got, BF16)
    moved = swap(to_chip, "dp", 2)
    query_grad = []
    for i in range(chunks):
        query_grad = parts[i].query(sent, stats, window(i), query_grad)
    query_grad = query_grad[0]
    moved = after(moved, query_grad, near_stats, far_stats)
    send, kept = keep_term(attn, grad_rows, pick(me, chip), shares, got, moved, count)

    pieces_of_keys = [(0, 2), (2, 1), (3, 1)]
    key_value = []
    stage = 0
    bit = 1
    while bit < count:
        moved = swap(send, "ctx", bit)
        if stage < len(pieces_of_keys):
            first, some = pieces_of_keys[stage]
            tied, send = lax.optimization_barrier((stats, send))
            sources = [(sent, tied), (near_sent, near_stats), (far_sent, far_stats)]
            held = mine[first * chunks // pairs]
            key_value = Attention(rows, width, chunks, first, some).key(held, sources, key_value)
            moved = after(moved, *key_value)
            stage += 1
        bit *= 2
        if bit < count:
            send, kept = halves(kept, moved, "ctx", bit)
    weight_grad = last_sum(kept[0], moved[0])
    key_grad, value_grad = key_value
    return query_grad[None], key_grad[None], value_grad[None], weight_grad


def solution(mesh):
    rows = P("dp", "ctx", None)
    return jax.shard_map(
        on_device,
        mesh=mesh,
        in_specs=(rows, rows, rows, P("dp", "ctx"), rows, P()),
        out_specs=(rows, rows, rows, P("ctx", "dp")),
        check_vma=False,
    )
```

```python
import functools

import jax
import jax.numpy as jnp
from jax import lax
from jax.experimental import pallas as pl
from jax.experimental.pallas import tpu as pltpu
from jax.sharding import PartitionSpec as P

HEAD_DIM = 64
TILE = 256
LANES = 128
TAG_LANES = 64
PIECES = 3
MASKED_SCORE = -1e30
SCALE = HEAD_DIM ** (-0.5)
F32 = jnp.float32
BF16 = jnp.bfloat16
PARAMS = pltpu.CompilerParams(vmem_limit_bytes=16 << 20)


def shift(x, by):
    size = lax.axis_size("ctx")
    pairs = [(i, i + by) for i in range(size) if 0 <= i + by < size]
    return lax.ppermute(x, "ctx", pairs)


def dot_t(a, b):
    return lax.dot_general(a, b, (((1,), (1,)), ((), ())), preferred_element_type=F32)


def dot(a, b):
    return jnp.dot(a, b, preferred_element_type=F32)


def lane_of(rows):
    return lax.broadcasted_iota(jnp.int32, (rows, LANES), 1)


def one_hot(tag_row):
    count = tag_row.shape[1]
    tag = lax.broadcasted_iota(jnp.int32, (LANES, count), 0) + 1
    hit = (tag_row.astype(F32) == tag.astype(F32)) & (tag <= TAG_LANES)
    return jnp.where(hit, 1.0, 0.0).astype(F32).T


def key_extra(tag_row):
    hot = one_hot(tag_row)
    lane = lane_of(hot.shape[0])
    return jnp.where(lane < TAG_LANES, (1.0 - hot) * MASKED_SCORE, 1.0).astype(BF16)


def pieces(x):
    out = []
    for _ in range(PIECES):
        part = x.astype(BF16).astype(F32)
        out.append(part)
        x = x - part
    return out


def own(lane, half):
    return (lane >= half * HEAD_DIM) & (lane < (half + 1) * HEAD_DIM)


def factor(chosen, value=1.0):
    return jnp.where(chosen, value, 0.0).astype(F32).astype(BF16)


def own_factor(half, value=1.0):
    return factor(own(lane_of(1), half), value)


def extra_factors(head):
    lane = lane_of(1)
    first = TAG_LANES + 2 * PIECES * head
    tag_lse = (lane < TAG_LANES) | ((lane >= first) & (lane < first + PIECES))
    delta = (lane >= first + PIECES) & (lane < first + 2 * PIECES)
    return factor(tag_lse), factor(delta)


def wide(features, extra):
    return jnp.concatenate([features, extra], axis=1)


def lower(shape, by_query):
    a = lax.broadcasted_iota(jnp.int32, shape, 0)
    b = lax.broadcasted_iota(jnp.int32, shape, 1)
    return (b <= a) if by_query else (a <= b)


def join(to_k, to_v, to_x, ke, ve, te, ko, vo, to, first_step):
    to_k[...] = ke[...] + ko[...]
    to_v[...] = ve[...] + vo[...]

    @pl.when(first_step)
    def _():
        to_x[...] = key_extra(te[0:1, :] + to[0:1, :])


def forward_kernel(first_pair, q_ref, g_ref, kc, vc, tc, ka, va, ta, ke, ve, te, ko, vo, to, *rest):
    before = rest[0] if first_pair else None
    o_ref, st_ref, xc, xa, xb, kb, vb, tag, rowed = rest[1 if first_pair else 0 :]
    step = pl.program_id(0)
    rows = q_ref.shape[0]

    @pl.when(step == 0)
    def _():
        xc[...] = key_extra(tc[0:1, :])
        xa[...] = key_extra(ta[0:1, :])
        tag[...] = one_hot(tc[0:1, :]).astype(BF16)
        rowed[...] = jnp.zeros_like(rowed)

    join(kb, vb, xb, ke, ve, te, ko, vo, to, step == 0)

    lane = lane_of(TILE)
    fold = lambda op, arrays: functools.reduce(
        op, [x[:, i : i + LANES] for x in arrays for i in range(0, x.shape[1], LANES)]
    )
    def score(base, half):
        end = base + TILE
        spans = [(ka, va, xa, base, rows), (kb, vb, xb, 0, rows)]
        spans += [(kc, vc, xc, 0, base)] if base else []
        spans += [(kc, vc, xc, base, end)]
        qx = wide(q_ref[base:end, :] * own_factor(half, SCALE), tag[base:end, :])
        scores = [dot_t(qx, wide(k[lo:hi, :], x[lo:hi, :])) for k, v, x, lo, hi in spans]
        scores[-1] = jnp.where(lower((TILE, TILE), True), scores[-1], MASKED_SCORE)
        return scores, spans

    turns = [(base, half) for base in range(0, rows, TILE) for half in range(2)]
    ahead = score(*turns[0])
    outs = []
    for turn, (base, half) in enumerate(turns):
        end = base + TILE
        scores, spans = ahead
        if turn + 1 < len(turns):
            ahead = score(*turns[turn + 1])
        mine = own(lane, half)
        peak = jnp.max(fold(jnp.maximum, scores), axis=1, keepdims=True)
        es = [jnp.exp(s - peak) for s in scores]
        total = jnp.sum(fold(jnp.add, es), axis=1, keepdims=True)
        acc = jnp.zeros((TILE, LANES), F32)
        for e, (k, v, x, lo, hi) in zip(es, spans):
            acc = acc + dot(e.astype(BF16), v[lo:hi, :])
        acc = acc * (1.0 / total)
        g = g_ref[base:end, :].astype(F32)
        delta = jnp.sum(jnp.where(mine, acc * g, 0.0), axis=1, keepdims=True)
        raw = raw if half else jnp.zeros((TILE, LANES), F32)
        for i, column in enumerate((peak, total, delta)):
            raw = jnp.where(lane == 3 * half + i, column, raw)
        outs.append(acc)
        if half == 0:
            continue
        o_ref[:, base:end] = jnp.where(own(lane, 0), outs[-2], outs[-1]).T.astype(BF16)
        turned = raw.T
        for side in range(2):
            peak, total, delta = (turned[3 * side + i : 3 * side + i + 1, :] for i in range(3))
            first = TAG_LANES + 2 * PIECES * (2 * (step + first_pair) + side)
            for i, part in enumerate(pieces(-(peak + jnp.log(total))) + pieces(-delta)):
                rowed[pl.ds(first + i, 1), base:end] = part

    @pl.when(step == pl.num_programs(0) - 1)
    def _():
        was = tag[...] if before is None else before[...]
        st_ref[...] = (was.astype(F32) + rowed[...].T).astype(BF16)


def query_kernel(first_pair, q_ref, g_ref, st_ref, kc, vc, tc, ka, va, ta, ke, ve, te, ko, vo, to, *rest):
    dq_ref, xc, xa, xb, kb, vb, acc, first = rest[1 if first_pair else 0 :]
    step = pl.program_id(0)
    rows = q_ref.shape[0]

    @pl.when(step == 0)
    def _():
        xc[...] = key_extra(tc[0:1, :])
        xa[...] = key_extra(ta[0:1, :])

    join(kb, vb, xb, ke, ve, te, ko, vo, to, step == 0)
    lane = lane_of(rows)
    q, g, stats = q_ref[...], g_ref[...], st_ref[...]
    for half in range(2):
        mine = own(lane, half)
        for_score, for_grad = extra_factors(2 * (step + first_pair) + half)
        qx = wide(q * own_factor(half, SCALE), stats * for_score)
        gx = wide(g * own_factor(half), stats * for_grad)
        acc[...] = jnp.zeros_like(acc)
        turns = [
            (k, v, x, near, lo)
            for k, v, x, near in ((ka, va, xa, 0), (kb, vb, xb, 1), (kc, vc, xc, 2))
            for lo in range(0, rows, TILE)
        ]

        def products(k, v, x, near, lo):
            hi = lo + TILE
            top = lo if near == 2 else 0
            end = hi if near == 0 else rows
            s = dot_t(qx[top:end], wide(k[lo:hi, :], x[lo:hi, :]))
            return s, dot_t(gx[top:end], wide(v[lo:hi, :], x[lo:hi, :])), top, end

        ahead = products(*turns[0])
        for turn, (k, v, x, near, lo) in enumerate(turns):
            s, dp, top, end = ahead
            if turn + 1 < len(turns):
                ahead = products(*turns[turn + 1])
            p = jnp.exp(s)
            if near == 2:
                p = jnp.where(lower((end - top, TILE), True), p, 0.0)
            acc[top:end, :] += dot((p * dp).astype(BF16), k[lo : lo + TILE, :])
        if half == 0:
            first[...] = acc[...]
        else:
            dq_ref[...] = (jnp.where(mine, acc[...], first[...]) * SCALE).astype(BF16)


def key_kernel(first_pair, k_ref, v_ref, t_ref, qc, gc, sc, qd, gd, sd, qe, ge, se, *rest):
    dk_ref, dv_ref, x_ref = rest[2 if first_pair else 0 :][:3]
    dks, dvs = rest[-4:-2], rest[-2:]
    step = pl.program_id(0)
    rows = k_ref.shape[0]

    @pl.when(step == 0)
    def _():
        x_ref[...] = key_extra(t_ref[0:1, :])

    kx = wide(k_ref[...], x_ref[...])
    vx = wide(v_ref[...], x_ref[...])
    for half in range(2):
        dk, dv = dks[half], dvs[half]
        dk[...] = jnp.zeros_like(dk)
        dv[...] = jnp.zeros_like(dv)
        for_score, for_grad = extra_factors(2 * (step + first_pair) + half)
        turns = [
            (q_ref, g_ref, s_ref, near, lo)
            for q_ref, g_ref, s_ref, near in ((qc, gc, sc, 2), (qd, gd, sd, 1), (qe, ge, se, 0))
            for lo in range(0, rows, TILE)
        ]

        def products(q_ref, g_ref, s_ref, near, lo):
            hi = lo + TILE
            top = lo if near == 0 else 0
            end = hi if near == 2 else rows
            q, g, stats = q_ref[lo:hi, :], g_ref[lo:hi, :], s_ref[lo:hi, :]
            qx = wide(q * own_factor(half, SCALE), stats * for_score)
            gx = wide(g * own_factor(half), stats * for_grad)
            return dot_t(kx[top:end], qx), dot_t(vx[top:end], gx), q, g, top, end

        ahead = products(*turns[0])
        for turn, (q_ref, g_ref, s_ref, near, lo) in enumerate(turns):
            s, dp, q, g, top, end = ahead
            if turn + 1 < len(turns):
                ahead = products(*turns[turn + 1])
            p = jnp.exp(s)
            if near == 2:
                row = lax.broadcasted_iota(jnp.int32, p.shape, 0)
                col = lax.broadcasted_iota(jnp.int32, p.shape, 1) + lo
                p = jnp.where(row <= col, p, 0.0)
            dv[top:end, :] += dot(p.astype(BF16), g)
            dk[top:end, :] += dot((p * dp).astype(BF16), q)
    second = own(lane_of(rows), 1)
    dk_ref[...] = (jnp.where(second, dks[1][...], dks[0][...]) * SCALE).astype(BF16)
    dv_ref[...] = jnp.where(second, dvs[1][...], dvs[0][...]).astype(BF16)


def lasting(microseconds):
    return pl.CostEstimate(flops=0, transcendentals=0, bytes_accessed=int(microseconds * 3.5e6))


class Attention:
    def __init__(self, rows, width, chunks, first, count):
        whole = width // LANES
        size = whole // chunks
        begin = first // size * size
        block = lambda off: pl.BlockSpec((rows, LANES), lambda p: (0, p + off))
        tag = pl.BlockSpec((16, rows), lambda p: (rows // 16, 0))
        self.first, self.count, self.rows, self.width = first, count, rows, width
        self.stat = pl.BlockSpec((rows, LANES), lambda p: (0, 0))
        self.sent = [block(first), block(whole + first)]
        self.held = [block(first - begin), block(size + first - begin), tag]
        self.out = block(first)
        self.extra = pltpu.VMEM((rows, LANES), BF16)
        self.total = pltpu.VMEM((rows, LANES), F32)

    def call(self, kernel, in_specs, args, out_specs, out_shape, scratch, before, aliased, last):
        before = list(before)
        spec = pl.BlockSpec(memory_space=pl.ANY) if aliased else self.stat
        aliases = {len(args) + i: i for i in range(len(before))} if aliased else {}
        return pl.pallas_call(
            functools.partial(kernel, self.first), grid=(self.count,),
            in_specs=in_specs + [spec] * len(before), out_specs=out_specs,
            out_shape=[jax.ShapeDtypeStruct(s, BF16) for s in out_shape],
            scratch_shapes=scratch, input_output_aliases=aliases,
            compiler_params=PARAMS, cost_estimate=lasting(last * self.count), name=kernel.__name__,
        )(*args, *before)

    def forward(self, sent, window, before):
        return self.call(
            forward_kernel, self.sent + self.held * 4,
            [sent, sent] + [x for x in window for _ in range(3)],
            [pl.BlockSpec((LANES, self.rows), lambda p: (p, 0)), self.stat],
            [(self.count * LANES, self.rows), (self.rows, LANES)],
            [self.extra] * 6 + [pltpu.VMEM((LANES, self.rows), F32)], before, False, 3.5,
        )

    def query(self, sent, stats, window, before):
        return self.call(
            query_kernel, self.sent + [self.stat] + self.held * 4,
            [sent, sent, stats] + [x for x in window for _ in range(3)],
            [self.out], [(self.rows, self.width)], [self.extra] * 5 + [self.total] * 2, before, True, 3.5,
        )

    def key(self, held, sources, before):
        return self.call(
            key_kernel, self.held + (self.sent + [self.stat]) * 3,
            [held] * 3 + [in_hbm(x) for q, st in sources for x in (q, q, st)],
            [self.out] * 2, [(self.rows, self.width)] * 2, [self.extra] + [self.total] * 4,
            before, True, 4.2,
        )


def send_kernel(q_ref, g_ref, w_ref, out_ref):
    half = pl.num_programs(0) // 2
    step = pl.program_id(0)

    @pl.when(step < half)
    def _():
        out_ref[...] = q_ref[...]

    @pl.when(step >= half)
    def _():
        out_ref[...] = dot_t(g_ref[...], w_ref[...]).astype(BF16)


def queries_to_send(query_rows, grad_rows, out_weight):
    rows, width = query_rows.shape
    model = grad_rows.shape[1]
    blocks = width // TILE
    return pl.pallas_call(
        send_kernel, grid=(2 * blocks,),
        in_specs=[
            pl.BlockSpec((rows, TILE), lambda i: (0, jnp.minimum(i, blocks - 1))),
            pl.BlockSpec((rows, model), lambda i: (0, 0)),
            pl.BlockSpec((TILE, model), lambda i: (jnp.maximum(i - blocks, 0), 0)),
        ],
        out_specs=pl.BlockSpec((rows, TILE), lambda i: (0, i)),
        out_shape=jax.ShapeDtypeStruct((rows, 2 * width), BF16),
        compiler_params=PARAMS, cost_estimate=lasting(5), name="queries_to_send",
    )(query_rows, grad_rows, out_weight)


def weight_kernel(sel_ref, *refs):
    outs, g_ref, w_ref = refs[:2], refs[2], refs[-1]
    size = outs[0].shape[0]
    for i, o_ref in enumerate(outs):
        part = dot(o_ref[...], g_ref[...])
        if len(refs) == 5:
            part = part + refs[3][0, i * size : (i + 1) * size, :].astype(F32)
        w_ref[0, i * size : (i + 1) * size, :] = part.astype(w_ref.dtype)


def weight_term(attn, grad_rows, columns, parts, got, dtype):
    size, rows = attn[0].shape
    width = size * len(attn)
    cols = grad_rows.shape[1] // parts
    steps = 1 if got is not None else parts // 2
    column = lambda i, s: (0, s[0] + 2 * i)
    extra = [] if got is None else [pl.BlockSpec((1, width, cols), lambda i, s: (s[1], 0, 0))]
    return pl.pallas_call(
        weight_kernel,
        grid_spec=pltpu.PrefetchScalarGridSpec(
            num_scalar_prefetch=1, grid=(steps,),
            in_specs=[pl.BlockSpec((size, rows), lambda i, s: (0, 0))] * 2
            + [pl.BlockSpec((rows, cols), column)] + extra,
            out_specs=pl.BlockSpec((1, width, cols), lambda i, s: (i, 0, 0)),
        ),
        out_shape=jax.ShapeDtypeStruct((steps, width, cols), dtype),
        compiler_params=PARAMS, cost_estimate=lasting(3), name="weight_term",
    )(columns, *map(in_hbm, attn), in_hbm(grad_rows), *([] if got is None else [got]))


def first_kernel(sel_ref, o_ref, g_ref, *rest):
    w_ref = rest[-1]
    w_ref[0] = dot(o_ref[...], g_ref[...]).astype(w_ref.dtype)


def first_term(attn, chunk, chunks, grad_rows, columns, parts, before):
    size, rows = attn.shape
    cols = grad_rows.shape[1] // parts
    return pl.pallas_call(
        first_kernel,
        grid_spec=pltpu.PrefetchScalarGridSpec(
            num_scalar_prefetch=1, grid=(parts // 2,),
            in_specs=[
                pl.BlockSpec((size, rows), lambda i, s: (0, 0)),
                pl.BlockSpec((rows, cols), lambda i, s: (0, s[0] + 2 * i)),
            ] + [pl.BlockSpec(memory_space=pl.ANY)] * len(before),
            out_specs=pl.BlockSpec((1, size, cols), lambda i, s: (i, chunk, 0)),
        ),
        out_shape=jax.ShapeDtypeStruct((parts // 2, size * chunks, cols), BF16),
        input_output_aliases={3: 0} if before else {},
        compiler_params=PARAMS, cost_estimate=lasting(2), name="first_term",
    )(columns, attn, in_hbm(grad_rows), *before)


def keep_kernel(sel_ref, o0_ref, o1_ref, g_ref, got_ref, moved_ref, send_ref, keep_ref):
    mine = sel_ref[2]
    count, size = send_ref.shape[0], send_ref.shape[1]
    half = o0_ref.shape[0]
    for i, o_ref in enumerate((o0_ref, o1_ref)):
        cut = slice(i * half, (i + 1) * half)
        part = dot(o_ref[...], g_ref[...]) + got_ref[0, cut, :].astype(F32) + moved_ref[0, cut, :].astype(F32)
        part = part.reshape(count // 2, 2, size, part.shape[1])
        low, high = part[:, 0], part[:, 1]
        out = slice(i * count // 2, (i + 1) * count // 2)
        send_ref[out] = jnp.where(mine == 0, high, low).astype(BF16)
        keep_ref[out] = jnp.where(mine == 0, low, high)


def keep_term(attn, grad_rows, columns, parts, got, moved, blocks):
    size, rows = attn[0].shape
    width = size * len(attn)
    cols = grad_rows.shape[1] // parts
    shape = (blocks // 2, width // blocks, cols)
    fixed = lambda shape: pl.BlockSpec(shape, lambda i, s: (0,) * len(shape))
    return pl.pallas_call(
        keep_kernel,
        grid_spec=pltpu.PrefetchScalarGridSpec(
            num_scalar_prefetch=1, grid=(1,),
            in_specs=[fixed((size, rows))] * 2 + [
                pl.BlockSpec((rows, cols), lambda i, s: (0, s[0])),
                pl.BlockSpec((1, width, cols), lambda i, s: (s[1], 0, 0)),
                fixed((1, width, cols)),
            ],
            out_specs=[fixed(shape)] * 2,
        ),
        out_shape=[jax.ShapeDtypeStruct(shape, BF16), jax.ShapeDtypeStruct(shape, F32)],
        compiler_params=PARAMS, cost_estimate=lasting(3), name="keep_term",
    )(columns, *map(in_hbm, attn), in_hbm(grad_rows), got, moved)


def swap(x, axis, bit):
    return lax.ppermute(x, axis, [(i, i ^ bit) for i in range(lax.axis_size(axis))])


def within_pair(x, to_odd):
    size = lax.axis_size("ctx")
    return lax.ppermute(x, "ctx", [(i, i + 1) if to_odd else (i + 1, i) for i in range(0, size, 2)])


def in_hbm(x):
    return pltpu.with_memory_space_constraint(x, pltpu.HBM)


def after(x, *others):
    return lax.optimization_barrier((x,) + others)[0]


def whole_of(x):
    return pl.BlockSpec(x.shape, lambda i, s: (0,) * x.ndim)


def stage_kernel(sel_ref, total_ref, got_ref, send_ref, keep_ref):
    mine = sel_ref[0]
    total = total_ref[...] + got_ref[...].astype(F32)
    total = total.reshape((send_ref.shape[0], 2) + send_ref.shape[1:])
    low, high = total[:, 0], total[:, 1]
    send_ref[...] = jnp.where(mine == 0, high, low).astype(BF16)
    keep_ref[...] = jnp.where(mine == 0, low, high)


def halves(total, got, axis, bit):
    mine = ((lax.axis_index(axis) // bit) % 2).astype(jnp.int32).reshape(1)
    out = lambda dtype: jax.ShapeDtypeStruct((total.shape[0] // 2,) + total.shape[1:], dtype)
    return pl.pallas_call(
        stage_kernel,
        grid_spec=pltpu.PrefetchScalarGridSpec(
            num_scalar_prefetch=1, grid=(1,), in_specs=[whole_of(total), whole_of(got)],
            out_specs=[whole_of(out(F32))] * 2,
        ),
        out_shape=[out(BF16), out(F32)],
        compiler_params=PARAMS, cost_estimate=lasting(1), name="stage",
    )(mine, total, got)


def last_kernel(total_ref, got_ref, out_ref):
    out_ref[...] = total_ref[...] + got_ref[...].astype(F32)


def last_sum(total, got):
    return pl.pallas_call(
        last_kernel, out_shape=jax.ShapeDtypeStruct(total.shape, F32),
        compiler_params=PARAMS, cost_estimate=lasting(1), name="last_sum",
    )(total, got)


def on_device(queries, keys, values, segment_ids, out_grad, out_weight):
    query_rows, key_rows, value_rows, grad_rows = queries[0], keys[0], values[0], out_grad[0]
    rows, width = query_rows.shape
    pairs = width // LANES
    chunks = 2
    size = width // chunks
    tag_rows = jnp.pad((segment_ids + 1).astype(BF16), ((0, 15), (0, 2 * size - rows)))
    odd = lax.axis_index("ctx") % 2 == 1
    mine, far, paired, passed = [], [], [], []
    for i in range(chunks):
        cut = slice(i * size, (i + 1) * size)
        tagged = after(tag_rows, *mine)
        mine.append(
            jnp.concatenate(
                [jnp.concatenate([key_rows[:, cut], value_rows[:, cut]], axis=1), tagged], axis=0
            )
        )
        far.append(shift(mine[i], 2))
    sent = queries_to_send(after(query_rows, *mine), grad_rows, out_weight)
    far[0] = after(far[0], sent)
    for i in range(chunks):
        paired.append(within_pair(mine[i], True))
        passed.append(within_pair(far[i], False))
    far_sent = shift(sent, -2)
    parts = [Attention(rows, width, chunks, i * pairs // chunks, pairs // chunks) for i in range(chunks)]
    window = lambda i: [mine[i], far[i], paired[i], passed[i]]
    shares = lax.axis_size("dp")
    count = lax.axis_size("ctx")
    me = lax.axis_index("dp").astype(jnp.int32)
    core, chip = me % 2, me // 2
    low = lax.axis_index("ctx").astype(jnp.int32) % 2
    pick = lambda part, entry: jnp.stack([part, entry, low])
    attn, stats, to_core = [], [], []
    from_forward = sent
    for i in range(chunks):
        half, after_half = parts[i].forward(from_forward, window(i), stats)
        attn.append(half)
        stats = [after_half]
        to_core = [first_term(half, i, chunks, grad_rows, pick(1 - core, core), shares, to_core)]
        if i == 0:
            relayed = jnp.where(odd, sent, after(far_sent, half))
            near_sent = swap(relayed, "ctx", 1)
            from_forward = after(sent, relayed, *to_core)
    stats = stats[0]
    near_stats = shift(stats, -1)
    far_stats = shift(stats, -2)

    got = swap(to_core[0], "dp", 1)
    to_chip = weight_term(attn, grad_rows, pick(2 * (1 - chip) + core, 1 - chip), shares, got, BF16)
    moved = swap(to_chip, "dp", 2)
    query_grad = []
    for i in range(chunks):
        query_grad = parts[i].query(sent, stats, window(i), query_grad)
    query_grad = query_grad[0]
    moved = after(moved, query_grad, near_stats, far_stats)
    send, kept = keep_term(attn, grad_rows, pick(me, chip), shares, got, moved, count)

    pieces_of_keys = [(0, 2), (2, 1), (3, 1)]
    key_value = []
    stage = 0
    bit = 1
    while bit < count:
        moved = swap(send, "ctx", bit)
        if stage < len(pieces_of_keys):
            first, some = pieces_of_keys[stage]
            tied, send = lax.optimization_barrier((stats, send))
            sources = [(sent, tied), (near_sent, near_stats), (far_sent, far_stats)]
            held = mine[first * chunks // pairs]
            key_value = Attention(rows, width, chunks, first, some).key(held, sources, key_value)
            moved = after(moved, *key_value)
            stage += 1
        bit *= 2
        if bit < count:
            send, kept = halves(kept, moved, "ctx", bit)
    weight_grad = last_sum(kept[0], moved[0])
    key_grad, value_grad = key_value
    return query_grad[None], key_grad[None], value_grad[None], weight_grad


def solution(mesh):
    rows = P("dp", "ctx", None)
    return jax.shard_map(
        on_device,
        mesh=mesh,
        in_specs=(rows, rows, rows, P("dp", "ctx"), rows, P()),
        out_specs=(rows, rows, rows, P("ctx", "dp")),
        check_vma=False,
    )
```

```python
import functools

import jax
import jax.numpy as jnp
from jax import lax
from jax.experimental import pallas as pl
from jax.experimental.pallas import tpu as pltpu
from jax.sharding import PartitionSpec as P

HEAD_DIM = 64
TILE = 256
LANES = 128
TAG_LANES = 64
PIECES = 3
MASKED_SCORE = -1e30
SCALE = HEAD_DIM ** (-0.5)
F32 = jnp.float32
BF16 = jnp.bfloat16
PARAMS = pltpu.CompilerParams(vmem_limit_bytes=16 << 20)


def shift(x, by):
    size = lax.axis_size("ctx")
    pairs = [(i, i + by) for i in range(size) if 0 <= i + by < size]
    return lax.ppermute(x, "ctx", pairs)


def dot_t(a, b):
    return lax.dot_general(a, b, (((1,), (1,)), ((), ())), preferred_element_type=F32)


def dot(a, b):
    return jnp.dot(a, b, preferred_element_type=F32)


def lane_of(rows):
    return lax.broadcasted_iota(jnp.int32, (rows, LANES), 1)


def one_hot(tag_row):
    count = tag_row.shape[1]
    tag = lax.broadcasted_iota(jnp.int32, (LANES, count), 0) + 1
    hit = (tag_row.astype(F32) == tag.astype(F32)) & (tag <= TAG_LANES)
    return jnp.where(hit, 1.0, 0.0).astype(F32).T


def key_extra(tag_row):
    hot = one_hot(tag_row)
    lane = lane_of(hot.shape[0])
    return jnp.where(lane < TAG_LANES, (1.0 - hot) * MASKED_SCORE, 1.0).astype(BF16)


def pieces(x):
    out = []
    for _ in range(PIECES):
        part = x.astype(BF16).astype(F32)
        out.append(part)
        x = x - part
    return out


def own(lane, half):
    return (lane >= half * HEAD_DIM) & (lane < (half + 1) * HEAD_DIM)


def factor(chosen, value=1.0):
    return jnp.where(chosen, value, 0.0).astype(F32).astype(BF16)


def own_factor(half, value=1.0):
    return factor(own(lane_of(1), half), value)


def extra_factors(head):
    lane = lane_of(1)
    first = TAG_LANES + 2 * PIECES * head
    tag_lse = (lane < TAG_LANES) | ((lane >= first) & (lane < first + PIECES))
    delta = (lane >= first + PIECES) & (lane < first + 2 * PIECES)
    return factor(tag_lse), factor(delta)


def wide(features, extra):
    return jnp.concatenate([features, extra], axis=1)


def lower(shape, by_query):
    a = lax.broadcasted_iota(jnp.int32, shape, 0)
    b = lax.broadcasted_iota(jnp.int32, shape, 1)
    return (b <= a) if by_query else (a <= b)


def join(to_k, to_v, to_x, ke, ve, te, ko, vo, to, first_step):
    to_k[...] = ke[...] + ko[...]
    to_v[...] = ve[...] + vo[...]

    @pl.when(first_step)
    def _():
        to_x[...] = key_extra(te[0:1, :] + to[0:1, :])


def forward_kernel(first_pair, q_ref, g_ref, kc, vc, tc, ka, va, ta, ke, ve, te, ko, vo, to, *rest):
    before = rest[0] if first_pair else None
    o_ref, st_ref, xc, xa, xb, kb, vb, tag, rowed = rest[1 if first_pair else 0 :]
    step = pl.program_id(0)
    rows = q_ref.shape[0]

    @pl.when(step == 0)
    def _():
        xc[...] = key_extra(tc[0:1, :])
        xa[...] = key_extra(ta[0:1, :])
        tag[...] = one_hot(tc[0:1, :]).astype(BF16)
        rowed[...] = jnp.zeros_like(rowed)

    join(kb, vb, xb, ke, ve, te, ko, vo, to, step == 0)

    lane = lane_of(TILE)
    fold = lambda op, arrays: functools.reduce(
        op, [x[:, i : i + LANES] for x in arrays for i in range(0, x.shape[1], LANES)]
    )
    def score(base, half):
        end = base + TILE
        spans = [(ka, va, xa, base, rows), (kb, vb, xb, 0, rows)]
        spans += [(kc, vc, xc, 0, base)] if base else []
        spans += [(kc, vc, xc, base, end)]
        qx = wide(q_ref[base:end, :] * own_factor(half, SCALE), tag[base:end, :])
        scores = [dot_t(qx, wide(k[lo:hi, :], x[lo:hi, :])) for k, v, x, lo, hi in spans]
        scores[-1] = jnp.where(lower((TILE, TILE), True), scores[-1], MASKED_SCORE)
        return scores, spans

    turns = [(base, half) for base in range(0, rows, TILE) for half in range(2)]
    ahead = score(*turns[0])
    outs = []
    for turn, (base, half) in enumerate(turns):
        end = base + TILE
        scores, spans = ahead
        if turn + 1 < len(turns):
            ahead = score(*turns[turn + 1])
        mine = own(lane, half)
        peak = jnp.max(fold(jnp.maximum, scores), axis=1, keepdims=True)
        es = [jnp.exp(s - peak) for s in scores]
        total = jnp.sum(fold(jnp.add, es), axis=1, keepdims=True)
        acc = jnp.zeros((TILE, LANES), F32)
        for e, (k, v, x, lo, hi) in zip(es, spans):
            acc = acc + dot(e.astype(BF16), v[lo:hi, :])
        acc = acc * (1.0 / total)
        g = g_ref[base:end, :].astype(F32)
        delta = jnp.sum(jnp.where(mine, acc * g, 0.0), axis=1, keepdims=True)
        raw = raw if half else jnp.zeros((TILE, LANES), F32)
        for i, column in enumerate((peak, total, delta)):
            raw = jnp.where(lane == 3 * half + i, column, raw)
        outs.append(acc)
        if half == 0:
            continue
        o_ref[:, base:end] = jnp.where(own(lane, 0), outs[-2], outs[-1]).T.astype(BF16)
        turned = raw.T
        for side in range(2):
            peak, total, delta = (turned[3 * side + i : 3 * side + i + 1, :] for i in range(3))
            first = TAG_LANES + 2 * PIECES * (2 * (step + first_pair) + side)
            for i, part in enumerate(pieces(-(peak + jnp.log(total))) + pieces(-delta)):
                rowed[pl.ds(first + i, 1), base:end] = part

    @pl.when(step == pl.num_programs(0) - 1)
    def _():
        was = tag[...] if before is None else before[...]
        st_ref[...] = (was.astype(F32) + rowed[...].T).astype(BF16)


def query_kernel(first_pair, q_ref, g_ref, st_ref, kc, vc, tc, ka, va, ta, ke, ve, te, ko, vo, to, *rest):
    dq_ref, xc, xa, xb, kb, vb, acc, first = rest[1 if first_pair else 0 :]
    step = pl.program_id(0)
    rows = q_ref.shape[0]

    @pl.when(step == 0)
    def _():
        xc[...] = key_extra(tc[0:1, :])
        xa[...] = key_extra(ta[0:1, :])

    join(kb, vb, xb, ke, ve, te, ko, vo, to, step == 0)
    lane = lane_of(rows)
    q, g, stats = q_ref[...], g_ref[...], st_ref[...]
    for half in range(2):
        mine = own(lane, half)
        for_score, for_grad = extra_factors(2 * (step + first_pair) + half)
        qx = wide(q * own_factor(half, SCALE), stats * for_score)
        gx = wide(g * own_factor(half), stats * for_grad)
        acc[...] = jnp.zeros_like(acc)
        turns = [
            (k, v, x, near, lo)
            for k, v, x, near in ((ka, va, xa, 0), (kb, vb, xb, 1), (kc, vc, xc, 2))
            for lo in range(0, rows, TILE)
        ]

        def products(k, v, x, near, lo):
            hi = lo + TILE
            top = lo if near == 2 else 0
            end = hi if near == 0 else rows
            s = dot_t(qx[top:end], wide(k[lo:hi, :], x[lo:hi, :]))
            return s, dot_t(gx[top:end], wide(v[lo:hi, :], x[lo:hi, :])), top, end

        ahead = products(*turns[0])
        for turn, (k, v, x, near, lo) in enumerate(turns):
            s, dp, top, end = ahead
            if turn + 1 < len(turns):
                ahead = products(*turns[turn + 1])
            p = jnp.exp(s)
            if near == 2:
                p = jnp.where(lower((end - top, TILE), True), p, 0.0)
            acc[top:end, :] += dot((p * dp).astype(BF16), k[lo : lo + TILE, :])
        if half == 0:
            first[...] = acc[...]
        else:
            dq_ref[...] = (jnp.where(mine, acc[...], first[...]) * SCALE).astype(BF16)


def key_kernel(first_pair, k_ref, v_ref, t_ref, qc, gc, sc, qd, gd, sd, qe, ge, se, *rest):
    dk_ref, dv_ref, x_ref = rest[2 if first_pair else 0 :][:3]
    dks, dvs = rest[-4:-2], rest[-2:]
    step = pl.program_id(0)
    rows = k_ref.shape[0]

    @pl.when(step == 0)
    def _():
        x_ref[...] = key_extra(t_ref[0:1, :])

    kx = wide(k_ref[...], x_ref[...])
    vx = wide(v_ref[...], x_ref[...])
    for half in range(2):
        dk, dv = dks[half], dvs[half]
        dk[...] = jnp.zeros_like(dk)
        dv[...] = jnp.zeros_like(dv)
        for_score, for_grad = extra_factors(2 * (step + first_pair) + half)
        turns = [
            (q_ref, g_ref, s_ref, near, lo)
            for q_ref, g_ref, s_ref, near in ((qc, gc, sc, 2), (qd, gd, sd, 1), (qe, ge, se, 0))
            for lo in range(0, rows, TILE)
        ]

        def products(q_ref, g_ref, s_ref, near, lo):
            hi = lo + TILE
            top = lo if near == 0 else 0
            end = hi if near == 2 else rows
            q, g, stats = q_ref[lo:hi, :], g_ref[lo:hi, :], s_ref[lo:hi, :]
            qx = wide(q * own_factor(half, SCALE), stats * for_score)
            gx = wide(g * own_factor(half), stats * for_grad)
            return dot_t(kx[top:end], qx), dot_t(vx[top:end], gx), q, g, top, end

        ahead = products(*turns[0])
        for turn, (q_ref, g_ref, s_ref, near, lo) in enumerate(turns):
            s, dp, q, g, top, end = ahead
            if turn + 1 < len(turns):
                ahead = products(*turns[turn + 1])
            p = jnp.exp(s)
            if near == 2:
                row = lax.broadcasted_iota(jnp.int32, p.shape, 0)
                col = lax.broadcasted_iota(jnp.int32, p.shape, 1) + lo
                p = jnp.where(row <= col, p, 0.0)
            dv[top:end, :] += dot(p.astype(BF16), g)
            dk[top:end, :] += dot((p * dp).astype(BF16), q)
    second = own(lane_of(rows), 1)
    dk_ref[...] = (jnp.where(second, dks[1][...], dks[0][...]) * SCALE).astype(BF16)
    dv_ref[...] = jnp.where(second, dvs[1][...], dvs[0][...]).astype(BF16)


def lasting(microseconds):
    return pl.CostEstimate(flops=0, transcendentals=0, bytes_accessed=int(microseconds * 3.5e6))


class Attention:
    def __init__(self, rows, width, chunks, first, count):
        whole = width // LANES
        size = whole // chunks
        begin = first // size * size
        block = lambda off: pl.BlockSpec((rows, LANES), lambda p: (0, p + off))
        tag = pl.BlockSpec((16, rows), lambda p: (rows // 16, 0))
        self.first, self.count, self.rows, self.width = first, count, rows, width
        self.stat = pl.BlockSpec((rows, LANES), lambda p: (0, 0))
        self.sent = [block(first), block(whole + first)]
        self.held = [block(first - begin), block(size + first - begin), tag]
        self.out = block(first)
        self.extra = pltpu.VMEM((rows, LANES), BF16)
        self.total = pltpu.VMEM((rows, LANES), F32)

    def call(self, kernel, in_specs, args, out_specs, out_shape, scratch, before, aliased, last):
        before = list(before)
        spec = pl.BlockSpec(memory_space=pl.ANY) if aliased else self.stat
        aliases = {len(args) + i: i for i in range(len(before))} if aliased else {}
        return pl.pallas_call(
            functools.partial(kernel, self.first), grid=(self.count,),
            in_specs=in_specs + [spec] * len(before), out_specs=out_specs,
            out_shape=[jax.ShapeDtypeStruct(s, BF16) for s in out_shape],
            scratch_shapes=scratch, input_output_aliases=aliases,
            compiler_params=PARAMS, cost_estimate=lasting(last * self.count), name=kernel.__name__,
        )(*args, *before)

    def forward(self, sent, window, before):
        return self.call(
            forward_kernel, self.sent + self.held * 4,
            [sent, sent] + [x for x in window for _ in range(3)],
            [pl.BlockSpec((LANES, self.rows), lambda p: (p, 0)), self.stat],
            [(self.count * LANES, self.rows), (self.rows, LANES)],
            [self.extra] * 6 + [pltpu.VMEM((LANES, self.rows), F32)], before, False, 3.5,
        )

    def query(self, sent, stats, window, before):
        return self.call(
            query_kernel, self.sent + [self.stat] + self.held * 4,
            [sent, sent, stats] + [x for x in window for _ in range(3)],
            [self.out], [(self.rows, self.width)], [self.extra] * 5 + [self.total] * 2, before, True, 3.5,
        )

    def key(self, held, sources, before):
        return self.call(
            key_kernel, self.held + (self.sent + [self.stat]) * 3,
            [held] * 3 + [y for q, st in sources for y in (in_hbm(q), in_hbm(q), st)],
            [self.out] * 2, [(self.rows, self.width)] * 2, [self.extra] + [self.total] * 4,
            before, True, 4.2,
        )


def send_kernel(q_ref, g_ref, w_ref, out_ref):
    half = pl.num_programs(0) // 2
    step = pl.program_id(0)

    @pl.when(step < half)
    def _():
        out_ref[...] = q_ref[...]

    @pl.when(step >= half)
    def _():
        out_ref[...] = dot_t(g_ref[...], w_ref[...]).astype(BF16)


def queries_to_send(query_rows, grad_rows, out_weight):
    rows, width = query_rows.shape
    model = grad_rows.shape[1]
    blocks = width // TILE
    return pl.pallas_call(
        send_kernel, grid=(2 * blocks,),
        in_specs=[
            pl.BlockSpec((rows, TILE), lambda i: (0, jnp.minimum(i, blocks - 1))),
            pl.BlockSpec((rows, model), lambda i: (0, 0)),
            pl.BlockSpec((TILE, model), lambda i: (jnp.maximum(i - blocks, 0), 0)),
        ],
        out_specs=pl.BlockSpec((rows, TILE), lambda i: (0, i)),
        out_shape=jax.ShapeDtypeStruct((rows, 2 * width), BF16),
        compiler_params=PARAMS, cost_estimate=lasting(5), name="queries_to_send",
    )(query_rows, grad_rows, out_weight)


def weight_kernel(sel_ref, *refs):
    outs, g_ref, w_ref = refs[:2], refs[2], refs[-1]
    size = outs[0].shape[0]
    for i, o_ref in enumerate(outs):
        part = dot(o_ref[...], g_ref[...])
        if len(refs) == 5:
            part = part + refs[3][0, i * size : (i + 1) * size, :].astype(F32)
        w_ref[0, i * size : (i + 1) * size, :] = part.astype(w_ref.dtype)


def weight_term(attn, grad_rows, columns, parts, got, dtype):
    size, rows = attn[0].shape
    width = size * len(attn)
    cols = grad_rows.shape[1] // parts
    steps = 1 if got is not None else parts // 2
    column = lambda i, s: (0, s[0] + 2 * i)
    extra = [] if got is None else [pl.BlockSpec((1, width, cols), lambda i, s: (s[1], 0, 0))]
    return pl.pallas_call(
        weight_kernel,
        grid_spec=pltpu.PrefetchScalarGridSpec(
            num_scalar_prefetch=1, grid=(steps,),
            in_specs=[pl.BlockSpec((size, rows), lambda i, s: (0, 0))] * 2
            + [pl.BlockSpec((rows, cols), column)] + extra,
            out_specs=pl.BlockSpec((1, width, cols), lambda i, s: (i, 0, 0)),
        ),
        out_shape=jax.ShapeDtypeStruct((steps, width, cols), dtype),
        compiler_params=PARAMS, cost_estimate=lasting(3), name="weight_term",
    )(columns, *map(in_hbm, attn), in_hbm(grad_rows), *([] if got is None else [got]))


def first_kernel(sel_ref, o_ref, g_ref, *rest):
    w_ref = rest[-1]
    w_ref[0] = dot(o_ref[...], g_ref[...]).astype(w_ref.dtype)


def first_term(attn, chunk, chunks, grad_rows, columns, parts, before):
    size, rows = attn.shape
    cols = grad_rows.shape[1] // parts
    return pl.pallas_call(
        first_kernel,
        grid_spec=pltpu.PrefetchScalarGridSpec(
            num_scalar_prefetch=1, grid=(parts // 2,),
            in_specs=[
                pl.BlockSpec((size, rows), lambda i, s: (0, 0)),
                pl.BlockSpec((rows, cols), lambda i, s: (0, s[0] + 2 * i)),
            ] + [pl.BlockSpec(memory_space=pl.ANY)] * len(before),
            out_specs=pl.BlockSpec((1, size, cols), lambda i, s: (i, chunk, 0)),
        ),
        out_shape=jax.ShapeDtypeStruct((parts // 2, size * chunks, cols), BF16),
        input_output_aliases={3: 0} if before else {},
        compiler_params=PARAMS, cost_estimate=lasting(2), name="first_term",
    )(columns, attn, in_hbm(grad_rows), *before)


def keep_kernel(sel_ref, o0_ref, o1_ref, g_ref, got_ref, moved_ref, send_ref, keep_ref):
    mine = sel_ref[2]
    count, size = send_ref.shape[0], send_ref.shape[1]
    half = o0_ref.shape[0]
    for i, o_ref in enumerate((o0_ref, o1_ref)):
        cut = slice(i * half, (i + 1) * half)
        part = dot(o_ref[...], g_ref[...]) + got_ref[0, cut, :].astype(F32) + moved_ref[0, cut, :].astype(F32)
        part = part.reshape(count // 2, 2, size, part.shape[1])
        low, high = part[:, 0], part[:, 1]
        out = slice(i * count // 2, (i + 1) * count // 2)
        send_ref[out] = jnp.where(mine == 0, high, low).astype(BF16)
        keep_ref[out] = jnp.where(mine == 0, low, high)


def keep_term(attn, grad_rows, columns, parts, got, moved, blocks):
    size, rows = attn[0].shape
    width = size * len(attn)
    cols = grad_rows.shape[1] // parts
    shape = (blocks // 2, width // blocks, cols)
    fixed = lambda shape: pl.BlockSpec(shape, lambda i, s: (0,) * len(shape))
    return pl.pallas_call(
        keep_kernel,
        grid_spec=pltpu.PrefetchScalarGridSpec(
            num_scalar_prefetch=1, grid=(1,),
            in_specs=[fixed((size, rows))] * 2 + [
                pl.BlockSpec((rows, cols), lambda i, s: (0, s[0])),
                pl.BlockSpec((1, width, cols), lambda i, s: (s[1], 0, 0)),
                fixed((1, width, cols)),
            ],
            out_specs=[fixed(shape)] * 2,
        ),
        out_shape=[jax.ShapeDtypeStruct(shape, BF16), jax.ShapeDtypeStruct(shape, F32)],
        compiler_params=PARAMS, cost_estimate=lasting(3), name="keep_term",
    )(columns, *map(in_hbm, attn), in_hbm(grad_rows), got, moved)


def swap(x, axis, bit):
    return lax.ppermute(x, axis, [(i, i ^ bit) for i in range(lax.axis_size(axis))])


def within_pair(x, to_odd):
    size = lax.axis_size("ctx")
    return lax.ppermute(x, "ctx", [(i, i + 1) if to_odd else (i + 1, i) for i in range(0, size, 2)])


def in_hbm(x):
    return pltpu.with_memory_space_constraint(x, pltpu.HBM)


def after(x, *others):
    return lax.optimization_barrier((x,) + others)[0]


def whole_of(x):
    return pl.BlockSpec(x.shape, lambda i, s: (0,) * x.ndim)


def stage_kernel(sel_ref, total_ref, got_ref, send_ref, keep_ref):
    mine = sel_ref[0]
    total = total_ref[...] + got_ref[...].astype(F32)
    total = total.reshape((send_ref.shape[0], 2) + send_ref.shape[1:])
    low, high = total[:, 0], total[:, 1]
    send_ref[...] = jnp.where(mine == 0, high, low).astype(BF16)
    keep_ref[...] = jnp.where(mine == 0, low, high)


def halves(total, got, axis, bit):
    mine = ((lax.axis_index(axis) // bit) % 2).astype(jnp.int32).reshape(1)
    out = lambda dtype: jax.ShapeDtypeStruct((total.shape[0] // 2,) + total.shape[1:], dtype)
    return pl.pallas_call(
        stage_kernel,
        grid_spec=pltpu.PrefetchScalarGridSpec(
            num_scalar_prefetch=1, grid=(1,), in_specs=[whole_of(total), whole_of(got)],
            out_specs=[whole_of(out(F32))] * 2,
        ),
        out_shape=[out(BF16), out(F32)],
        compiler_params=PARAMS, cost_estimate=lasting(1), name="stage",
    )(mine, total, got)


def last_kernel(total_ref, got_ref, out_ref):
    out_ref[...] = total_ref[...] + got_ref[...].astype(F32)


def last_sum(total, got):
    return pl.pallas_call(
        last_kernel, out_shape=jax.ShapeDtypeStruct(total.shape, F32),
        compiler_params=PARAMS, cost_estimate=lasting(1), name="last_sum",
    )(total, got)


def on_device(queries, keys, values, segment_ids, out_grad, out_weight):
    query_rows, key_rows, value_rows, grad_rows = queries[0], keys[0], values[0], out_grad[0]
    rows, width = query_rows.shape
    pairs = width // LANES
    chunks = 2
    size = width // chunks
    tag_rows = jnp.pad((segment_ids + 1).astype(BF16), ((0, 15), (0, 2 * size - rows)))
    odd = lax.axis_index("ctx") % 2 == 1
    mine, far, paired, passed = [], [], [], []
    for i in range(chunks):
        cut = slice(i * size, (i + 1) * size)
        tagged = after(tag_rows, *mine)
        mine.append(
            jnp.concatenate(
                [jnp.concatenate([key_rows[:, cut], value_rows[:, cut]], axis=1), tagged], axis=0
            )
        )
        far.append(shift(mine[i], 2))
    sent = queries_to_send(after(query_rows, *mine), grad_rows, out_weight)
    far[0] = after(far[0], sent)
    for i in range(chunks):
        paired.append(within_pair(mine[i], True))
        passed.append(within_pair(far[i], False))
    far_sent = shift(sent, -2)
    parts = [Attention(rows, width, chunks, i * pairs // chunks, pairs // chunks) for i in range(chunks)]
    window = lambda i: [mine[i], far[i], paired[i], passed[i]]
    shares = lax.axis_size("dp")
    count = lax.axis_size("ctx")
    me = lax.axis_index("dp").astype(jnp.int32)
    core, chip = me % 2, me // 2
    low = lax.axis_index("ctx").astype(jnp.int32) % 2
    pick = lambda part, entry: jnp.stack([part, entry, low])
    attn, stats, to_core = [], [], []
    from_forward = sent
    for i in range(chunks):
        half, after_half = parts[i].forward(from_forward, window(i), stats)
        attn.append(half)
        stats = [after_half]
        to_core = [first_term(half, i, chunks, grad_rows, pick(1 - core, core), shares, to_core)]
        if i == 0:
            relayed = jnp.where(odd, sent, after(far_sent, half))
            near_sent = swap(relayed, "ctx", 1)
            from_forward = after(sent, relayed, *to_core)
    stats = stats[0]
    near_stats = shift(stats, -1)
    far_stats = shift(stats, -2)

    got = swap(to_core[0], "dp", 1)
    to_chip = weight_term(attn, grad_rows, pick(2 * (1 - chip) + core, 1 - chip), shares, got, BF16)
    moved = swap(to_chip, "dp", 2)
    query_grad = []
    for i in range(chunks):
        query_grad = parts[i].query(sent, stats, window(i), query_grad)
    query_grad = query_grad[0]
    moved = after(moved, query_grad, near_stats, far_stats)
    send, kept = keep_term(attn, grad_rows, pick(me, chip), shares, got, moved, count)

    pieces_of_keys = [(0, 2), (2, 1), (3, 1)]
    key_value = []
    stage = 0
    bit = 1
    while bit < count:
        moved = swap(send, "ctx", bit)
        if stage < len(pieces_of_keys):
            first, some = pieces_of_keys[stage]
            tied, send = lax.optimization_barrier((stats, send))
            sources = [(sent, tied), (near_sent, near_stats), (far_sent, far_stats)]
            held = mine[first * chunks // pairs]
            key_value = Attention(rows, width, chunks, first, some).key(held, sources, key_value)
            moved = after(moved, *key_value)
            stage += 1
        bit *= 2
        if bit < count:
            send, kept = halves(kept, moved, "ctx", bit)
    weight_grad = last_sum(kept[0], moved[0])
    key_grad, value_grad = key_value
    return query_grad[None], key_grad[None], value_grad[None], weight_grad


def solution(mesh):
    rows = P("dp", "ctx", None)
    return jax.shard_map(
        on_device,
        mesh=mesh,
        in_specs=(rows, rows, rows, P("dp", "ctx"), rows, P()),
        out_specs=(rows, rows, rows, P("ctx", "dp")),
        check_vma=False,
    )
```
